128 devices in a mesh: mem: 8 (over z_hi, y), sp: 16 (over x, z_lo, core).
Axes of the slice: x: 4, y: 4, z: 4 (z_hi: 2, z_lo: 2; z = z_hi * 2 + z_lo), core: 2. Of those that a mesh axis runs over, the one named last changes fastest.
Arguments:
- member_predictors: bfloat16 [64, 8, 32, 128], P('mem', None, 'sp'), may hold values from -6 to 6
- member_skill_logit: bfloat16 [64, 32, 128], P('mem', 'sp'), may hold values from -8 to 250
- opening_filter: bfloat16 [9, 8, 128], replicated, may hold values from -0.75 to 0.75
- opening_bias: float32 [128], replicated, may hold values from -3 to 3
- following_filter: bfloat16 [9, 128, 128], replicated, may hold values from -0.1875 to 0.1875
- layer_norm_scales: float32 [2, 2, 128], replicated, may hold values from 0.5 to 1.5
- query_key_value_weight: bfloat16 [2, 128, 384], replicated, may hold values from -0.5 to 0.5
- attention_output_weight: bfloat16 [2, 128, 128], replicated, may hold values from -0.5 to 0.5
- upward_weight: bfloat16 [2, 128, 512], replicated, may hold values from -0.5 to 0.5
- downward_weight: bfloat16 [2, 512, 128], replicated, may hold values from -0.25 to 0.25
- closing_norm_scale: float32 [128], replicated, may hold values from 0.5 to 1.5
- readout_weight: bfloat16 [128, 2], replicated, may hold values from -0.5 to 0.5
Outputs:
- corrected: float32 [64, 2, 32, 128], P('mem', None, 'sp')
The draws below stay inside these ranges and needn't reach their ends.
All inputs are finite; a program needn't handle non-finite values.
Results may differ from the reference program's by a relative error of at most 0.012.
Values may be sent and summed in bfloat16 or wider, within the bound.
No kernel may reach another device: no remote copies, remote signals or barrier semaphores. Data moves between devices by JAX's collectives and lax.ppermute only.
A program may use at most 64 MiB of HBM per device.

```python
import math
import jax
import jax.numpy as jnp
from jax import lax

PREDICTOR_COUNT = 8
CORRECTED_COUNT = 2
E = 128
HEADS = 8
FF = 512
LAYERS = 2
GRID_COLUMNS = 128
MEMBER_COUNT = 64
GRID_ROWS = 32


def draw_member_skill_logit(key, part):
    baseline = jnp.clip(1.5 * jax.random.normal(jax.random.fold_in(key, 11), (MEMBER_COUNT, GRID_ROWS, GRID_COLUMNS), jnp.float32), -8.0, 8.0)
    return baseline.astype(jnp.bfloat16)


def level_of(key, extent, cuts, least, high):
    level = 1.0
    for axis_at, shards_of in cuts:
        steps = jax.random.uniform(jax.random.fold_in(jax.random.fold_in(key, 6), axis_at), (shards_of,), jnp.float32, least / len(cuts), high / len(cuts))
        level = level * jnp.repeat(jnp.exp(steps), extent[axis_at] // shards_of).reshape((-1,) + (1,) * (len(extent) - 1 - axis_at))
    return level


def gaussian(key, extent, deviation, reach, pieces=(), dtype=jnp.bfloat16):
    entries = jax.random.normal(key, extent, jnp.float32) * deviation
    if len(pieces) > 0:
        entries = level_of(key, extent, pieces, -0.22, 0.18) * entries
    return jnp.clip(entries, min=-reach, max=reach).astype(dtype)


def setup_inputs(seed: int = 0) -> dict:
    key_list = jax.random.split(jax.random.key(seed), 13)
    return {
        "member_predictors": gaussian(key_list[0], (MEMBER_COUNT, PREDICTOR_COUNT, GRID_ROWS, GRID_COLUMNS), 1.0, 6.0, ((0, 8), (2, 16))),
        "member_skill_logit": draw_member_skill_logit(jax.random.fold_in(key_list[12], 71), 0),
        "opening_filter": gaussian(key_list[2], (9, PREDICTOR_COUNT, E), (9 * PREDICTOR_COUNT) ** -0.5, 0.75),
        "opening_bias": gaussian(key_list[3], (E,), 0.5, 3.0, (), jnp.float32),
        "following_filter": gaussian(key_list[4], (9, E, E), (9 * E) ** -0.5, 0.1875),
        "layer_norm_scales": jnp.clip(1.0 + 0.1 * jax.random.normal(key_list[5], (LAYERS, 2, E), jnp.float32), 0.5, 1.5),
        "query_key_value_weight": gaussian(key_list[6], (LAYERS, E, 3 * E), E ** -0.5, 0.5),
        "attention_output_weight": gaussian(key_list[7], (LAYERS, E, E), E ** -0.5, 0.5),
        "upward_weight": gaussian(key_list[8], (LAYERS, E, FF), E ** -0.5, 0.5),
        "downward_weight": gaussian(key_list[9], (LAYERS, FF, E), FF ** -0.5, 0.25),
        "closing_norm_scale": jnp.clip(1.0 + 0.1 * jax.random.normal(key_list[10], (E,), jnp.float32), 0.5, 1.5),
        "readout_weight": gaussian(key_list[11], (E, CORRECTED_COUNT), E ** -0.5, 0.5),
    }


def layer_norm(stream, scaling):
    average = lax.optimization_barrier(jnp.mean(stream, -1, keepdims=True))
    centred = stream - average
    variance = lax.optimization_barrier(jnp.mean(centred * centred, -1, keepdims=True))
    return centred * lax.rsqrt(variance + 1e-05) * scaling

def conv_fields(border_padded, kernel):
    row_count = border_padded.shape[2] - 2
    col_count = border_padded.shape[3] - 2
    summed = jnp.zeros((border_padded.shape[0], row_count, col_count, kernel.shape[2]), jnp.float32)
    for stencil in range(9):
        row_off = stencil // 3
        col_off = stencil % 3
        shifted = border_padded[:, :, row_off:row_off + row_count, col_off:col_off + col_count]
        summed = summed + jnp.einsum('mchw,ce->mhwe', shifted.astype(jnp.float32), kernel[stencil].astype(jnp.float32))
    return summed

def conv_features(border_padded, kernel):
    row_count = border_padded.shape[1] - 2
    col_count = border_padded.shape[2] - 2
    summed = jnp.zeros((border_padded.shape[0], row_count, col_count, kernel.shape[2]), jnp.float32)
    for stencil in range(9):
        row_off = stencil // 3
        col_off = stencil % 3
        shifted = border_padded[:, row_off:row_off + row_count, col_off:col_off + col_count, :]
        summed = summed + jnp.einsum('mhwe,ef->mhwf', shifted.astype(jnp.float32), kernel[stencil].astype(jnp.float32))
    return summed

def members_attend(stream, logits, layer_norm_scales, query_key_value_weight, attention_output_weight, upward_weight, downward_weight, closing_norm_scale, readout_weight):
    blocks, members, width = stream.shape
    head_size = width // HEADS
    for layer in range(LAYERS):
        normed = layer_norm(stream, layer_norm_scales[layer, 0]).astype(jnp.bfloat16)
        triple = jnp.dot(normed.reshape(-1, width), query_key_value_weight[layer], preferred_element_type=jnp.float32).astype(jnp.bfloat16)
        triple = triple.reshape(blocks, members, 3, HEADS, head_size)
        queries = triple[:, :, 0].astype(jnp.float32)
        keys = triple[:, :, 1].astype(jnp.float32)
        values = triple[:, :, 2].astype(jnp.float32)
        scores = jnp.einsum('bqhd,bkhd->bhqk', queries, keys) / math.sqrt(head_size)
        scores = scores + logits.astype(jnp.float32)[:, None, None, :]
        highest = lax.optimization_barrier(jnp.max(scores, -1, keepdims=True))
        raised = jnp.exp(scores - highest)
        weights = (raised / lax.optimization_barrier(jnp.sum(raised, -1, keepdims=True))).astype(jnp.bfloat16)
        attended = jnp.einsum('bhqk,bkhd->bqhd', weights.astype(jnp.float32), values).astype(jnp.bfloat16)
        stream = stream + jnp.dot(attended.reshape(-1, width), attention_output_weight[layer], preferred_element_type=jnp.float32).reshape(blocks, members, width)
        normed = layer_norm(stream, layer_norm_scales[layer, 1]).astype(jnp.bfloat16)
        hidden = jax.nn.gelu(jnp.dot(normed.reshape(-1, width), upward_weight[layer], preferred_element_type=jnp.float32)).astype(jnp.bfloat16)
        stream = stream + jnp.dot(hidden, downward_weight[layer], preferred_element_type=jnp.float32).reshape(blocks, members, width)
    final = layer_norm(stream, closing_norm_scale).astype(jnp.bfloat16)
    return jnp.dot(final.reshape(-1, width), readout_weight, preferred_element_type=jnp.float32).reshape(blocks, members, readout_weight.shape[1])

def reference(member_predictors, member_skill_logit, opening_filter, opening_bias, following_filter, layer_norm_scales, query_key_value_weight, attention_output_weight, upward_weight, downward_weight, closing_norm_scale, readout_weight):

    def embed_member_fields(member_fields):
        border_padded = jnp.pad(member_fields, ((0, 0), (1, 1), (1, 1)))[None]
        first = jax.nn.gelu(conv_fields(border_padded, opening_filter) + opening_bias).astype(jnp.bfloat16)
        padded_first = jnp.pad(first, ((0, 0), (1, 1), (1, 1), (0, 0)))
        summed = first.astype(jnp.float32) + conv_features(padded_first, following_filter)
        return summed.astype(jnp.bfloat16)[0]
    member_features = lax.map(embed_member_fields, member_predictors)
    members = member_features.shape[0]
    cells = GRID_ROWS * GRID_COLUMNS
    block = math.gcd(cells, 64)
    stream = member_features.transpose(1, 2, 0, 3).reshape(cells // block, block, members, E)
    logit_blocks = member_skill_logit.transpose(1, 2, 0).reshape(cells // block, block, members)

    def one_block(packed):
        return members_attend(packed[0].astype(jnp.float32), packed[1], layer_norm_scales, query_key_value_weight, attention_output_weight, upward_weight, downward_weight, closing_norm_scale, readout_weight)
    field_adjustment = lax.map(one_block, (stream, logit_blocks))
    field_adjustment = field_adjustment.reshape(GRID_ROWS, GRID_COLUMNS, members, CORRECTED_COUNT).transpose(2, 3, 0, 1)
    return member_predictors[:, :CORRECTED_COUNT].astype(jnp.float32) + field_adjustment
```

```python
import math

import jax
import jax.numpy as jnp
from jax import lax
from jax.experimental import pallas as pl
from jax.experimental.pallas import tpu as pltpu
from jax.sharding import PartitionSpec as P

HEADS = 8
LAYERS = 2
WIDTH = 128
FF = 512
FIELDS = 8
OUT_FIELDS = 2
LANES = 128
SLOT = 32
EPS = 1e-05
LOG2E = math.log2(math.e)
GELU_A = math.sqrt(2.0 / math.pi)
GELU_B = GELU_A * 0.044715
VMEM_LIMIT = 60 * 1024 * 1024

F32 = jnp.float32
BF16 = jnp.bfloat16
NT = (((1,), (1,)), ((), ()))


def iota(shape, dim):
    return lax.broadcasted_iota(jnp.int32, shape, dim)


def matmul(a, b):
    return jnp.dot(a, b, preferred_element_type=F32)


def gelu(x):
    half = 0.5 * x
    return half + half * jnp.tanh(x * (GELU_A + GELU_B * (x * x)))


def pack_kernel(up_ref, own_ref, down_ref, logit_ref, out_ref):
    i = iota((LANES, LANES), 0)
    k = iota((LANES, LANES), 1)
    order = (k == (i % 8) * 16 + (i // 16) * 2 + (i // 8) % 2).astype(F32).astype(BF16)
    c = iota((LANES, 8 * SLOT), 0)
    lane = iota((LANES, 8 * SLOT), 1)
    dest = lane // SLOT
    j = lane % SLOT
    pick = ((c == 16 * dest - 2 + j) & (j < 20)).astype(F32).astype(BF16)
    pick_logit = [
        ((c == 16 * dest + 8 * g + j - 24) & (j >= 24)).astype(F32).astype(BF16) for g in range(2)
    ]
    li = iota((16, 16), 0)
    lk = iota((16, 16), 1)
    order_logit = (lk == (li % 8) * 2 + li // 8).astype(F32).astype(BF16)
    ordered_logit = matmul(order_logit, logit_ref[...]).astype(BF16)
    logit_parts = [matmul(ordered_logit, pick_logit[g]) for g in range(2)]
    part = iota((16, LANES), 1) // SLOT
    for s, ref in enumerate((up_ref, own_ref, down_ref)):
        picked = matmul(matmul(order, ref[...]).astype(BF16), pick)
        for q in range(2):
            for h in range(2):
                rolled = []
                for b in range(4):
                    f = 4 * h + b
                    piece = picked[f * 16 : f * 16 + 16, q * LANES : (q + 1) * LANES]
                    if s == 1 and f < 2:
                        piece = piece + logit_parts[f][:, q * LANES : (q + 1) * LANES]
                    rolled.append(
                        [piece] + [pltpu.roll(piece, SLOT * d, 1) for d in range(1, 4)]
                    )
                for a in range(4):
                    row = rolled[0][(0 - a) % 4]
                    for b in range(1, 4):
                        row = jnp.where(part == b, rolled[b][(b - a) % 4], row)
                    out_ref[4 * q + a, s * 16 : s * 16 + 16, h * LANES : (h + 1) * LANES] = (
                        row.astype(BF16)
                    )


def prepare_kernel(
    opening_ref, bias_ref, following_ref, scales_ref, closing_ref, qkv_ref, out_w_ref, up_w_ref,
    down_w_ref, readout_ref,
    band_ref, bias_out, following_out, scales_out, qkv_out, out_w_out, up_w_out, down_w_out,
    readout_out,
):
    def flip(value):
        return value.astype(F32).T.astype(BF16)

    def column(row):
        return jnp.broadcast_to(row, (LANES, LANES)).T

    t = iota((72, 3 * 256), 0)
    lane = iota((72, 3 * 256), 1)
    tap = t // 8
    f = t % 8
    place = (
        (lane // 256 == tap // 3) & ((lane % 256) // SLOT == f) & (lane % SLOT == tap % 3)
    )
    flat = opening_ref[...].astype(F32).reshape(72, WIDTH)
    base = matmul(flat.T.astype(BF16), place.astype(F32).astype(BF16))
    for c in range(18):
        for q in range(6):
            piece = base[:, q * LANES : (q + 1) * LANES]
            if c:
                piece = pltpu.roll(piece, c, 1)
            band_ref[c, :, q * LANES : (q + 1) * LANES] = piece.astype(BF16)
    bias_out[...] = column(bias_ref[...])
    for tap in range(9):
        following_out[:, tap * WIDTH : (tap + 1) * WIDTH] = flip(following_ref[tap])
    for layer in range(LAYERS):
        for n in range(2):
            scales_out[2 * layer + n] = column(scales_ref[2 * layer + n : 2 * layer + n + 1])
        for n in range(3):
            qkv_out[layer, n * WIDTH : (n + 1) * WIDTH] = flip(
                qkv_ref[layer, :, n * WIDTH : (n + 1) * WIDTH]
            )
        out_w_out[layer] = flip(out_w_ref[layer])
        for n in range(FF // WIDTH):
            cut = slice(n * WIDTH, (n + 1) * WIDTH)
            up_w_out[layer, cut] = flip(up_w_ref[layer, :, cut])
            down_w_out[layer, :, cut] = flip(down_w_ref[layer, cut])
    scales_out[2 * LAYERS] = column(closing_ref[...])
    turned = readout_ref[...].astype(F32).T
    readout_out[...] = jnp.concatenate(
        [turned, jnp.zeros((16 - OUT_FIELDS, WIDTH), F32)], axis=0
    ).astype(BF16)


def main_kernel(
    message_ref, band_ref, bias_ref, following_ref, scales_ref, qkv_ref, out_w_ref, up_w_ref,
    down_w_ref, readout_ref, result_ref, first_ref, logit_ref, read_ref,
    *, columns, pairs
):
    mem = lax.axis_index("mem")
    sp = lax.axis_index("sp")
    low = iota((WIDTH, LANES), 1) < 64

    rows = []
    for s in range(3):
        block = message_ref[:, s * 16 : (s + 1) * 16, :].astype(F32).reshape(8, 2, 8, 256)
        for r in range(2):
            rows.append(block[:, r].reshape(64, 256))
    for p in range(16):
        lane = 24 + p if p < 8 else SLOT + 24 + p - 8
        spread = jnp.concatenate(
            [jnp.broadcast_to(rows[2 + r][:, lane : lane + 1], (64, 64)) for r in range(2)], axis=1
        )
        logit_ref[p] = spread * LOG2E
    taken = [row.astype(BF16) for row in rows]
    window = jnp.concatenate(
        [
            jnp.concatenate([taken[1 + d], taken[2 + d], taken[d], taken[3 + d]], axis=0)
            for d in range(3)
        ],
        axis=1,
    )
    outer = jnp.where(
        low, jnp.where(sp > 0, 1.0, 0.0), jnp.where(sp < lax.axis_size("sp") - 1, 1.0, 0.0)
    )
    bias = bias_ref[...]

    def open_columns(step, carry):
        start = step * columns
        summed = lax.dot_general(
            band_ref[pl.ds(start, columns)].reshape(columns * WIDTH, 3 * 256),
            window,
            NT,
            preferred_element_type=F32,
        )
        for n in range(columns):
            c = start + n
            inside = ((c > 0) | (mem > 0)) & ((c < 17) | (mem < lax.axis_size("mem") - 1))
            keep = jnp.where(inside, 1.0, 0.0)
            part = summed[n * WIDTH : (n + 1) * WIDTH]
            inner_rows = gelu(part[:, :LANES] + bias) * keep
            outer_rows = gelu(part[:, LANES:] + bias) * (outer * keep)
            swapped = pltpu.roll(inner_rows, 64, 1)
            first_ref[0, c] = jnp.where(low, outer_rows, swapped).astype(BF16)
            first_ref[1, c] = inner_rows.astype(BF16)
            first_ref[2, c] = jnp.where(low, swapped, outer_rows).astype(BF16)
        return carry

    lax.fori_loop(0, 18 // columns, open_columns, 0)

    head_row = iota((HEADS * 64, WIDTH), 0) // 64
    head_lane = iota((HEADS * 64, WIDTH), 1) // 16
    key_mask = (head_row == head_lane).astype(F32).astype(BF16)
    value_mask = (
        (iota((64, 256), 0) // 16 == iota((64, 256), 1) // 64).astype(F32).astype(BF16)
    )
    scales = [
        jnp.concatenate([scales_ref[n]] * pairs, axis=1) for n in range(2 * LAYERS + 1)
    ]

    def norm(stream, scale):
        centred = stream - jnp.mean(stream, 0, keepdims=True)
        variance = jnp.mean(centred * centred, 0, keepdims=True)
        return (centred * lax.rsqrt(variance + EPS) * scale).astype(BF16)

    def lanes_of(value, n):
        return value[:, n * LANES : (n + 1) * LANES]

    def attend_columns(step, carry):
        start = step * pairs
        taps = []
        for d in range(3):
            for e in range(3):
                taps.append(
                    jnp.concatenate([first_ref[d, start + n + e] for n in range(pairs)], axis=1)
                )
        stream = matmul(following_ref[...], jnp.concatenate(taps, axis=0))
        stream = (stream + taps[4].astype(F32)).astype(BF16).astype(F32)
        for layer in range(LAYERS):
            normed = norm(stream, scales[2 * layer])
            triple = matmul(qkv_ref[layer], normed)
            attended = []
            for n in range(pairs):
                part = lanes_of(triple, n)
                query = part[:WIDTH] * (LOG2E / 4.0)
                query = jnp.concatenate(
                    [jnp.where(low, query, 0.0), jnp.where(low, 0.0, query)], axis=0
                ).astype(BF16)
                key = part[WIDTH : 2 * WIDTH].T.astype(BF16)
                value = part[2 * WIDTH :]
                turned = pltpu.roll(value, 64, 1)
                values = [
                    jnp.where(low, value, turned).astype(BF16),
                    jnp.where(low, turned, value).astype(BF16),
                ]
                keys = jnp.concatenate(
                    [jnp.concatenate([key[64 * r : 64 * r + 64]] * HEADS, 0) * key_mask for r in range(2)],
                    axis=1,
                )
                scores = matmul(keys, query).reshape(HEADS, 64, LANES) + logit_ref[start + n][None]
                highest = jnp.max(scores, 1, keepdims=True)
                raised = jnp.exp2(scores - highest).astype(BF16).reshape(2, 256, LANES)
                for half in range(2):
                    spread = [
                        jnp.concatenate([v[64 * half : 64 * half + 64]] * 2, 1) * value_mask
                        for v in values
                    ]
                    found = matmul(
                        jnp.concatenate(spread + [value_mask], axis=0), raised[half]
                    )
                    attended.append(
                        (jnp.where(low[:64], found[:64], found[64:128]) / found[128:]).astype(BF16)
                    )
            attended = jnp.concatenate(
                [
                    jnp.concatenate(attended[2 * n : 2 * n + 2], axis=0) for n in range(pairs)
                ],
                axis=1,
            )
            stream = stream + matmul(out_w_ref[layer], attended)
            normed = norm(stream, scales[2 * layer + 1])
            hidden = gelu(matmul(up_w_ref[layer], normed)).astype(BF16)
            stream = stream + matmul(down_w_ref[layer], hidden)
        final = norm(stream, scales[2 * LAYERS])
        correction = matmul(readout_ref[...], final)
        for n in range(pairs):
            for f in range(OUT_FIELDS):
                read_ref[pl.ds(f * 16 + start + n, 1), :] = lanes_of(correction, n)[f : f + 1]
        return carry

    lax.fori_loop(0, 16 // pairs, attend_columns, 0)

    turned = jnp.concatenate([read_ref[...], jnp.zeros((LANES - 32, LANES), F32)], axis=0).T
    result = turned[:64] + pltpu.roll(turned[64:], 32, 1)
    result_ref[...] = result.reshape(8, 8, LANES)


def unpack_kernel(got_ref, own_ref, out_ref):
    i = iota((32, LANES), 0)
    k = iota((32, LANES), 1)
    order = (k == (i % 8) * 16 + i // 8).astype(F32).astype(BF16)
    fields = matmul(order, own_ref[...])
    part = iota((8, LANES), 1) // 16
    for f in range(OUT_FIELDS):
        for r in range(2):
            n = 2 * f + r
            total = fields[n * 8 : n * 8 + 8]
            for source in range(8):
                shift = (16 * source - (r * 32 + f * 16)) % LANES
                piece = got_ref[source]
                if shift:
                    piece = pltpu.roll(piece, shift, 1)
                total = total + jnp.where(part == source, piece, 0.0)
            out_ref[:, n, :] = total


def call(kernel, out_shape, args, scratch=()):
    return pl.pallas_call(
        kernel,
        out_shape=out_shape,
        scratch_shapes=list(scratch),
        compiler_params=pltpu.CompilerParams(vmem_limit_bytes=VMEM_LIMIT),
    )(*args)


def shape(dims, dtype):
    return jax.ShapeDtypeStruct(dims, dtype)


def shards(
    member_predictors,
    member_skill_logit,
    opening_filter,
    opening_bias,
    following_filter,
    layer_norm_scales,
    query_key_value_weight,
    attention_output_weight,
    upward_weight,
    downward_weight,
    closing_norm_scale,
    readout_weight,
):
    own = member_predictors.reshape(LANES, LANES)
    ends = lax.axis_size("sp") - 1
    above = lax.ppermute(own, "sp", [(i, i + 1) for i in range(ends)])
    below = lax.ppermute(own, "sp", [(i + 1, i) for i in range(ends)])
    message = call(
        pack_kernel,
        shape((8, 48, 256), BF16),
        (above, own, below, member_skill_logit.reshape(16, LANES)),
    )
    arrived = lax.all_to_all(message, "mem", 0, 0, tiled=True)
    prepared = call(
        prepare_kernel,
        (
            shape((18, WIDTH, 3 * 256), BF16),
            shape((WIDTH, LANES), F32),
            shape((WIDTH, 9 * WIDTH), BF16),
            shape((2 * LAYERS + 1, WIDTH, LANES), F32),
            shape((LAYERS, 3 * WIDTH, WIDTH), BF16),
            shape((LAYERS, WIDTH, WIDTH), BF16),
            shape((LAYERS, FF, WIDTH), BF16),
            shape((LAYERS, WIDTH, FF), BF16),
            shape((16, WIDTH), BF16),
        ),
        (
            opening_filter,
            opening_bias.reshape(1, WIDTH),
            following_filter,
            layer_norm_scales.reshape(2 * LAYERS, WIDTH),
            closing_norm_scale.reshape(1, WIDTH),
            query_key_value_weight,
            attention_output_weight,
            upward_weight,
            downward_weight,
            readout_weight,
        ),
    )

    def main(*refs):
        main_kernel(*refs, columns=6, pairs=2)

    result = call(
        main,
        shape((8, 8, LANES), F32),
        (arrived,) + tuple(prepared),
        (
            pltpu.VMEM((3, 18, WIDTH, LANES), BF16),
            pltpu.VMEM((16, 64, LANES), F32),
            pltpu.VMEM((32, LANES), F32),
        ),
    )
    got = lax.all_to_all(result, "mem", 0, 0, tiled=True)
    output = call(unpack_kernel, shape((8, 4, LANES), F32), (got, own))
    return output.reshape(8, OUT_FIELDS, 2, LANES)


def solution(mesh):
    in_specs = (
        P("mem", None, "sp", None),
        P("mem", "sp", None),
        P(),
        P(),
        P(),
        P(),
        P(),
        P(),
        P(),
        P(),
        P(),
        P(),
    )
    out_specs = P("mem", None, "sp", None)
    return jax.shard_map(shards, mesh=mesh, in_specs=in_specs, out_specs=out_specs, check_vma=False)
```

```python
import math

import jax
import jax.numpy as jnp
from jax import lax
from jax.experimental import pallas as pl
from jax.experimental.pallas import tpu as pltpu
from jax.sharding import PartitionSpec as P

HEADS = 8
LAYERS = 2
WIDTH = 128
FF = 512
FIELDS = 8
OUT_FIELDS = 2
LANES = 128
SLOT = 16
WINDOW = 9
EPS = 1e-05
LOG2E = math.log2(math.e)
GELU_A = math.sqrt(2.0 / math.pi)
GELU_B = GELU_A * 0.044715

PACK_LIMIT = 8
MAIN_LIMIT = 48
UNPACK_LIMIT = 8

F32 = jnp.float32
BF16 = jnp.bfloat16
NT = (((1,), (1,)), ((), ()))


def iota(shape, dim):
    return lax.broadcasted_iota(jnp.int32, shape, dim)


def matmul(a, b):
    return jnp.dot(a, b, preferred_element_type=F32)


def exact(condition):
    return condition.astype(F32).astype(BF16)


def gelu(x):
    half = 0.5 * x
    return half + half * jnp.tanh(x * (GELU_A + GELU_B * (x * x)))


def pack_kernel(up_ref, down_ref, own_hbm, logit_hbm, out_ref, own_ref, logit_ref, sems):
    copies = [
        pltpu.make_async_copy(own_hbm, own_ref, sems.at[0]),
        pltpu.make_async_copy(logit_hbm, logit_ref, sems.at[1]),
    ]
    for copy in copies:
        copy.start()
    i = iota((LANES, LANES), 0)
    k = iota((LANES, LANES), 1)
    order = exact(k == (i % 8) * 16 + (i // 16) * 2 + (i // 8) % 2)
    c = iota((LANES, 2 * LANES), 0)
    lane = iota((LANES, 2 * LANES), 1)
    dest = lane // 32
    j = lane % SLOT
    second = (lane // SLOT) % 2
    pick = exact((c == 16 * dest - 2 + 9 * second + j) & (j < 11))
    masks = [(iota((16, LANES), 1) // SLOT // (1 << bit)) % 2 == 0 for bit in range(3)]
    for s in (0, 2, 1):
        if s == 1:
            for copy in copies:
                copy.wait()
        ref = (up_ref, own_ref, down_ref)[s]
        picked = matmul(matmul(order, ref[...]).astype(BF16), pick)
        if s == 1:
            li = iota((16, 16), 0)
            lk = iota((16, 16), 1)
            ordered = matmul(exact(lk == (li % 8) * 2 + li // 8), logit_ref[...]).astype(BF16)
        for q in range(2):
            blocks = []
            for f in range(FIELDS):
                block = picked[f * 16 : f * 16 + 16, q * LANES : (q + 1) * LANES]
                if s == 1:
                    spot = (c == 16 * dest + 2 * f + j - 12) & (j >= 12) & (j < 14) & (second == 0)
                    spot = exact(spot[:, q * LANES : (q + 1) * LANES])
                    block = block + matmul(ordered, spot)
                blocks.append(block)
            for bit in range(3):
                step = 1 << bit
                shift = SLOT * step
                for f in range(FIELDS):
                    if f & step == 0:
                        first, other = blocks[f], blocks[f + step]
                        blocks[f] = jnp.where(masks[bit], first, pltpu.roll(other, shift, 1))
                        blocks[f + step] = jnp.where(
                            masks[bit], pltpu.roll(first, LANES - shift, 1), other
                        )
            for n in range(8):
                at = (n % 2) * LANES
                out_ref[4 * q + n // 2, s * 16 : s * 16 + 16, at : at + LANES] = blocks[n].astype(
                    BF16
                )


def prepare_kernel(
    opening_ref, bias_ref, following_ref, scales_ref, closing_ref, qkv_ref, out_w_ref, up_w_ref,
    down_w_ref, readout_ref,
    band_ref, bias_out, following_out, scales_out, qkv_out, out_w_out, up_w_out, down_w_out,
    readout_out,
):
    def flip(value):
        return value.astype(F32).T.astype(BF16)

    def column(row):
        return jnp.broadcast_to(row, (LANES, LANES)).T

    t = iota((72, 3 * LANES), 0)
    lane = iota((72, 3 * LANES), 1)
    tap = t // 8
    place = exact(
        (lane // LANES == tap // 3)
        & ((lane % LANES) // SLOT == t % 8)
        & (lane % SLOT == tap % 3)
    )
    flat = opening_ref[...].astype(F32).reshape(72, WIDTH)
    base = matmul(flat.T.astype(BF16), place)
    for c in range(WINDOW):
        for d in range(3):
            piece = base[:, d * LANES : (d + 1) * LANES]
            if c:
                piece = pltpu.roll(piece, c, 1)
            band_ref[c * WIDTH : (c + 1) * WIDTH, d * LANES : (d + 1) * LANES] = piece.astype(BF16)
    bias_out[...] = column(bias_ref[...])
    for tap in range(9):
        following_out[:, tap * WIDTH : (tap + 1) * WIDTH] = flip(following_ref[tap])
    for layer in range(LAYERS):
        for n in range(2):
            scales_out[2 * layer + n] = column(scales_ref[2 * layer + n : 2 * layer + n + 1])
        for n in range(3):
            qkv_out[layer, n * WIDTH : (n + 1) * WIDTH] = flip(
                qkv_ref[layer, :, n * WIDTH : (n + 1) * WIDTH]
            )
        out_w_out[layer] = flip(out_w_ref[layer])
        for n in range(FF // WIDTH):
            cut = slice(n * WIDTH, (n + 1) * WIDTH)
            up_w_out[layer, cut] = flip(up_w_ref[layer, :, cut])
            down_w_out[layer, :, cut] = flip(down_w_ref[layer, cut])
    scales_out[2 * LAYERS] = column(closing_ref[...])
    turned = readout_ref[...].astype(F32).T
    readout_out[...] = jnp.concatenate(
        [turned, jnp.zeros((16 - OUT_FIELDS, WIDTH), F32)], axis=0
    ).astype(BF16)


def main_kernel(message_ref, *refs, pairs, lag):
    held_refs, refs = refs[: len(HELD)], refs[len(HELD) :]
    result_ref, first_ref, logit_ref, read_ref = refs[:4]
    local_refs, sems = refs[4:-1], refs[-1]
    copies = [
        pltpu.make_async_copy(held_refs[n], local_refs[n], sems.at[n]) for n in range(len(HELD))
    ]
    for copy in copies:
        copy.start()
    (
        band_ref, bias_ref, following_ref, scales_ref, qkv_ref, out_w_ref, up_w_ref, down_w_ref,
        readout_ref,
    ) = local_refs
    mem = lax.axis_index("mem")
    sp = lax.axis_index("sp")
    low = iota((WIDTH, LANES), 1) < 64

    rows = []
    for s in range(3):
        block = message_ref[:, s * 16 : (s + 1) * 16, :].astype(F32).reshape(8, 2, 8, 256)
        for r in range(2):
            rows.append(block[:, r].reshape(64, 256))
    for p in range(16):
        lane = (p // 2) * SLOT + 12 + p % 2
        spread = jnp.concatenate(
            [jnp.broadcast_to(rows[2 + r][:, lane : lane + 1], (64, 64)) for r in range(2)], axis=1
        )
        logit_ref[p] = spread * LOG2E
    taken = [row.astype(BF16) for row in rows]
    windows = [
        jnp.concatenate(
            [
                jnp.concatenate([taken[1 + d], taken[2 + d], taken[d], taken[3 + d]], axis=0)[
                    :, g * LANES : (g + 1) * LANES
                ]
                for d in range(3)
            ],
            axis=1,
        )
        for g in range(2)
    ]
    outer = jnp.where(
        low, jnp.where(sp > 0, 1.0, 0.0), jnp.where(sp < lax.axis_size("sp") - 1, 1.0, 0.0)
    )
    left = jnp.where(mem > 0, 1.0, 0.0)
    right = jnp.where(mem < lax.axis_size("mem") - 1, 1.0, 0.0)
    copies[0].wait()
    copies[1].wait()
    bias = bias_ref[...]

    for g in range(2):
        for start in range(0, WINDOW, 3):
            summed = lax.dot_general(
                band_ref[start * WIDTH : (start + 3) * WIDTH],
                windows[g],
                NT,
                preferred_element_type=F32,
            )
            for n in range(3):
                c = g * WINDOW + start + n
                part = summed[n * WIDTH : (n + 1) * WIDTH]
                inner_rows = gelu(part[:, :LANES] + bias)
                outer_rows = gelu(part[:, LANES:] + bias) * outer
                if c in (0, 2 * WINDOW - 1):
                    inner_rows = inner_rows * (right if c else left)
                    outer_rows = outer_rows * (right if c else left)
                swapped = pltpu.roll(inner_rows, 64, 1)
                first_ref[0, c] = jnp.where(low, outer_rows, swapped).astype(BF16)
                first_ref[1, c] = inner_rows.astype(BF16)
                first_ref[2, c] = jnp.where(low, swapped, outer_rows).astype(BF16)

    for copy in copies[2:]:
        copy.wait()
    head_row = iota((HEADS * 64, WIDTH), 0) // 64
    head_lane = iota((HEADS * 64, WIDTH), 1) // 16
    key_mask = (head_row == head_lane).astype(F32).astype(BF16)
    value_mask = (
        (iota((64, 256), 0) // 16 == iota((64, 256), 1) // 64).astype(F32).astype(BF16)
    )
    scales = [scales_ref[n] for n in range(2 * LAYERS + 1)]

    def norm(stream, scale):
        parts = []
        for n in range(pairs):
            part = lanes_of(stream, n)
            centred = part - jnp.mean(part, 0, keepdims=True)
            variance = jnp.mean(centred * centred, 0, keepdims=True)
            parts.append((centred * lax.rsqrt(variance + EPS) * scale).astype(BF16))
        return jnp.concatenate(parts, axis=1)

    def lanes_of(value, n):
        return value[:, n * LANES : (n + 1) * LANES]

    groups = 16 // pairs
    streams = {}
    kept = {}

    def follow(group):
        taps = []
        for d in range(3):
            for e in range(3):
                taps.append(
                    jnp.concatenate(
                        [first_ref[d, group * pairs + n + e] for n in range(pairs)], axis=1
                    )
                )
        stream = matmul(following_ref[...], jnp.concatenate(taps, axis=0))
        streams[group] = (stream + taps[4].astype(F32)).astype(BF16).astype(F32)

    def project(layer, group):
        normed = norm(streams[group], scales[2 * layer])
        kept[group, "triple"] = matmul(qkv_ref[layer], normed)

    def split(group, n):
        part = lanes_of(kept[group, "triple"], n)
        query = part[:WIDTH] * (LOG2E / 4.0)
        query = jnp.concatenate(
            [jnp.where(low, query, 0.0), jnp.where(low, 0.0, query)], axis=0
        ).astype(BF16)
        key = part[WIDTH : 2 * WIDTH].T.astype(BF16)
        value = part[2 * WIDTH :]
        turned = pltpu.roll(value, 64, 1)
        values = [
            jnp.where(low, value, turned).astype(BF16),
            jnp.where(low, turned, value).astype(BF16),
        ]
        kept[group, n] = query, key, values

    def score(group, n, half):
        query, key, _ = kept[group, n]
        mask = key_mask[256 * half : 256 * half + 256]
        keys = jnp.concatenate(
            [jnp.concatenate([key[64 * r : 64 * r + 64]] * 4, axis=0) * mask for r in range(2)],
            axis=1,
        )
        kept[group, n, half] = matmul(keys, query).reshape(4, 64, LANES)

    def soften(group, n, half):
        scores = kept[group, n, half] + logit_ref[group * pairs + n][None]
        highest = jnp.max(scores, 1, keepdims=True)
        kept[group, n, half] = jnp.exp2(scores - highest).astype(BF16).reshape(256, LANES)

    def gather(group, n, half):
        values = kept[group, n][2]
        spread = [
            jnp.concatenate([v[64 * half : 64 * half + 64]] * 2, axis=1) * value_mask
            for v in values
        ]
        found = matmul(
            jnp.concatenate(spread + [value_mask], axis=0), kept[group, n, half]
        )
        kept[group, n, half] = (
            jnp.where(low[:64], found[:64], found[64:128]) / found[128:]
        ).astype(BF16)

    def attend(layer, group):
        attended = jnp.concatenate(
            [
                jnp.concatenate([kept[group, n, half] for half in range(2)], axis=0)
                for n in range(pairs)
            ],
            axis=1,
        )
        streams[group] = streams[group] + matmul(out_w_ref[layer], attended)

    def renorm(layer, group):
        kept[group, "normed"] = norm(streams[group], scales[2 * layer + 1])

    def widen(layer, group, q):
        cut = slice(q * WIDTH, (q + 1) * WIDTH)
        kept[group, "hidden", q] = matmul(up_w_ref[layer, cut], kept[group, "normed"])

    def bend(group, q):
        kept[group, "hidden", q] = gelu(kept[group, "hidden", q]).astype(BF16)

    def narrow(layer, group):
        hidden = jnp.concatenate(
            [kept[group, "hidden", q] for q in range(FF // WIDTH)], axis=0
        )
        streams[group] = streams[group] + matmul(down_w_ref[layer], hidden)

    def read(group):
        correction = matmul(readout_ref[...], norm(streams[group], scales[2 * LAYERS]))
        for n in range(pairs):
            for f in range(OUT_FIELDS):
                at = f * 16 + group * pairs + n
                read_ref[at : at + 1, :] = lanes_of(correction, n)[f : f + 1]

    issue = []
    slots = 2 * pairs
    for layer in range(LAYERS):
        for group in range(groups):
            base = (layer * groups + group) * slots

            def add(offset, step, *arguments, base=base):
                issue.append((base + offset, len(issue), step, arguments))

            if layer == 0:
                add(-2, follow, group)
            add(0, project, layer, group)
            at = 2
            for n in range(pairs):
                add(at + 2 * n, split, group, n)
                for half in range(2):
                    k = at + 2 * n + half
                    add(k + lag[0], score, group, n, half)
                    add(k + lag[0] + lag[1], soften, group, n, half)
                    add(k + lag[0] + lag[1] + lag[2], gather, group, n, half)
            at = at + slots - 1 + sum(lag[:3]) + 1
            add(at, attend, layer, group)
            add(at + 1, renorm, layer, group)
            for q in range(4):
                add(at + 2 + q, widen, layer, group, q)
                add(at + 2 + q + lag[3], bend, group, q)
            at = at + 2 + 3 + lag[3] + 1
            add(at, narrow, layer, group)
            if layer == LAYERS - 1:
                add(at + 1, read, group)
    issue.sort(key=lambda entry: entry[:2])
    for _, _, step, arguments in issue:
        step(*arguments)

    turned = jnp.concatenate([read_ref[...], jnp.zeros((LANES - 32, LANES), F32)], axis=0).T
    result = turned[:64] + pltpu.roll(turned[64:], 32, 1)
    result_ref[...] = result.reshape(8, 8, LANES)


def unpack_kernel(got_ref, own_ref, out_ref):
    i = iota((32, LANES), 0)
    k = iota((32, LANES), 1)
    order = (k == (i % 8) * 16 + i // 8).astype(F32).astype(BF16)
    fields = matmul(order, own_ref[...])
    part = iota((8, LANES), 1) // 16
    for f in range(OUT_FIELDS):
        for r in range(2):
            n = 2 * f + r
            total = fields[n * 8 : n * 8 + 8]
            for source in range(8):
                shift = (16 * source - (r * 32 + f * 16)) % LANES
                piece = got_ref[source]
                if shift:
                    piece = pltpu.roll(piece, shift, 1)
                total = total + jnp.where(part == source, piece, 0.0)
            out_ref[:, n, :] = total


HELD = (
    ((WINDOW * WIDTH, 3 * LANES), BF16),
    ((WIDTH, LANES), F32),
    ((WIDTH, 9 * WIDTH), BF16),
    ((2 * LAYERS + 1, WIDTH, LANES), F32),
    ((LAYERS, 3 * WIDTH, WIDTH), BF16),
    ((LAYERS, WIDTH, WIDTH), BF16),
    ((LAYERS, FF, WIDTH), BF16),
    ((LAYERS, WIDTH, FF), BF16),
    ((16, WIDTH), BF16),
)
IN_VMEM = pl.BlockSpec(memory_space=pltpu.VMEM)
IN_HBM = pl.BlockSpec(memory_space=pltpu.HBM)


def call(kernel, out_shape, args, limit, in_specs=None, scratch=()):
    return pl.pallas_call(
        kernel,
        out_shape=out_shape,
        in_specs=in_specs or [pl.BlockSpec()] * len(args),
        scratch_shapes=list(scratch),
        compiler_params=pltpu.CompilerParams(vmem_limit_bytes=limit * 1024 * 1024),
    )(*args)


def shape(dims, dtype):
    return jax.ShapeDtypeStruct(dims, dtype)


def in_hbm(value):
    return pltpu.with_memory_space_constraint(value, pltpu.HBM)


def main_call(arrived, prepared, **options):
    def main(*refs):
        main_kernel(*refs, **options)

    return call(
        main,
        shape((8, 8, LANES), F32),
        (arrived,) + tuple(in_hbm(each) for each in prepared),
        MAIN_LIMIT,
        [pl.BlockSpec()] + [IN_HBM] * len(HELD),
        [
            pltpu.VMEM((3, 2 * WINDOW, WIDTH, LANES), BF16),
            pltpu.VMEM((16, 64, LANES), F32),
            pltpu.VMEM((32, LANES), F32),
        ]
        + [pltpu.VMEM(*each) for each in HELD]
        + [pltpu.SemaphoreType.DMA((len(HELD),))],
    )


def shards(
    member_predictors,
    member_skill_logit,
    opening_filter,
    opening_bias,
    following_filter,
    layer_norm_scales,
    query_key_value_weight,
    attention_output_weight,
    upward_weight,
    downward_weight,
    closing_norm_scale,
    readout_weight,
):
    own = member_predictors.reshape(LANES, LANES)
    ends = lax.axis_size("sp") - 1
    above = lax.ppermute(own, "sp", [(i, i + 1) for i in range(ends)])
    below = lax.ppermute(own, "sp", [(i + 1, i) for i in range(ends)])
    message = call(
        pack_kernel,
        shape((8, 48, 256), BF16),
        (above, below, in_hbm(own), in_hbm(member_skill_logit.reshape(16, LANES))),
        PACK_LIMIT,
        [pl.BlockSpec()] * 2 + [IN_HBM] * 2,
        (
            pltpu.VMEM((LANES, LANES), BF16),
            pltpu.VMEM((16, LANES), BF16),
            pltpu.SemaphoreType.DMA((2,)),
        ),
    )
    arrived = lax.all_to_all(message, "mem", 0, 0, tiled=True)
    prepared = call(
        prepare_kernel,
        tuple(shape(*each) for each in HELD),
        (
            opening_filter,
            opening_bias.reshape(1, WIDTH),
            following_filter,
            layer_norm_scales.reshape(2 * LAYERS, WIDTH),
            closing_norm_scale.reshape(1, WIDTH),
            query_key_value_weight,
            attention_output_weight,
            upward_weight,
            downward_weight,
            readout_weight,
        ),
        60,
    )

    result = main_call(arrived, prepared, pairs=4, lag=(1, 2, 2, 1))
    got = lax.all_to_all(result, "mem", 0, 0, tiled=True)
    output = call(unpack_kernel, shape((8, 4, LANES), F32), (got, own), UNPACK_LIMIT)
    return output.reshape(8, OUT_FIELDS, 2, LANES)


def solution(mesh):
    in_specs = (
        P("mem", None, "sp", None),
        P("mem", "sp", None),
        P(),
        P(),
        P(),
        P(),
        P(),
        P(),
        P(),
        P(),
        P(),
        P(),
    )
    out_specs = P("mem", None, "sp", None)
    return jax.shard_map(shards, mesh=mesh, in_specs=in_specs, out_specs=out_specs, check_vma=False)
```

```python
import math

import jax
import jax.numpy as jnp
from jax import lax
from jax.experimental import pallas as pl
from jax.experimental.pallas import tpu as pltpu
from jax.sharding import PartitionSpec as P

LAYERS = 2
WIDTH = 128
FF = 512
FIELDS = 8
OUT_FIELDS = 2
LANES = 128
SLOT = 16
COLUMNS = 8
WINDOW = COLUMNS + 2
CELL_PAIRS = 2 * COLUMNS
EPS = 1e-05
LOG2E = math.log2(math.e)
GELU_A = math.sqrt(2.0 / math.pi)
GELU_B = GELU_A * 0.044715

PACK_LIMIT = 8
MAIN_LIMIT = 48
UNPACK_LIMIT = 8

F32 = jnp.float32
BF16 = jnp.bfloat16
NT = (((1,), (1,)), ((), ()))


def iota(shape, dim):
    return lax.broadcasted_iota(jnp.int32, shape, dim)


def matmul(a, b):
    return jnp.dot(a, b, preferred_element_type=F32)


def exact(condition):
    return condition.astype(F32).astype(BF16)


def gelu(half):
    return half + half * jnp.tanh(half * (2.0 * GELU_A + 8.0 * GELU_B * (half * half)))


def pack_kernel(other_ref, own_hbm, logit_hbm, out_ref, own_ref, logit_ref, sems):
    copies = [
        pltpu.make_async_copy(own_hbm, own_ref, sems.at[0]),
        pltpu.make_async_copy(logit_hbm, logit_ref, sems.at[1]),
    ]
    for copy in copies:
        copy.start()
    i = iota((LANES, LANES), 0)
    k = iota((LANES, LANES), 1)
    order = exact(k == (i % 8) * 16 + (i // 16) * 2 + (i // 8) % 2)
    li = iota((16, 16), 0)
    lk = iota((16, 16), 1)
    order_logit = exact(lk == (li % 8) * 2 + li // 8)
    c = iota((LANES, 2 * LANES), 0)
    lane = iota((LANES, 2 * LANES), 1)
    dest = lane // SLOT
    j = lane % SLOT
    pick = exact((c == COLUMNS * dest - 2 + j) & (j < 12))
    stretch = exact((c == COLUMNS * dest + j) & (j < COLUMNS))
    spot = iota((16, LANES), 1) % SLOT == 12
    masks = [(iota((16, LANES), 1) // SLOT // (1 << bit)) % 2 == 0 for bit in range(3)]
    for s in (1, 0):
        if s == 0:
            for copy in copies:
                copy.wait()
            logits = matmul(matmul(order_logit, logit_ref[...]).astype(BF16), stretch)
        ref = (own_ref, other_ref)[s]
        picked = matmul(matmul(order, ref[...]).astype(BF16), pick)
        for q in range(2):
            cut = slice(q * LANES, (q + 1) * LANES)
            blocks = []
            for f in range(FIELDS):
                block = picked[f * 16 : f * 16 + 16, cut]
                if s == 0:
                    block = jnp.where(spot, pltpu.roll(logits[:, cut], 12 - f, 1), block)
                blocks.append(block)
            for bit in range(3):
                step = 1 << bit
                shift = SLOT * step
                for f in range(FIELDS):
                    if f & step == 0:
                        first, other = blocks[f], blocks[f + step]
                        blocks[f] = jnp.where(masks[bit], first, pltpu.roll(other, shift, 1))
                        blocks[f + step] = jnp.where(
                            masks[bit], pltpu.roll(first, LANES - shift, 1), other
                        )
            for n in range(8):
                out_ref[8 * q + n, s * 16 : s * 16 + 16, :] = blocks[n].astype(BF16)


def prepare_kernel(
    opening_ref, bias_ref, following_ref, scales_ref, closing_ref, qkv_ref, out_w_ref, up_w_ref,
    down_w_ref, readout_ref,
    band_ref, bias_out, following_out, scales_out, qkv_out, out_w_out, up_w_out, down_w_out,
    readout_out,
):
    def flip(value):
        return value.astype(F32).T.astype(BF16)

    def column(row):
        return jnp.broadcast_to(row, (LANES, LANES)).T

    t = iota((72, 3 * LANES), 0)
    lane = iota((72, 3 * LANES), 1)
    tap = t // 8
    place = exact(
        (lane // LANES == tap // 3)
        & ((lane % LANES) // SLOT == t % 8)
        & (lane % SLOT == tap % 3)
    )
    flat = opening_ref[...].astype(F32).reshape(72, WIDTH)
    base = 0.5 * matmul(flat.T.astype(BF16), place)
    for c in range(WINDOW):
        for d in range(3):
            piece = base[:, d * LANES : (d + 1) * LANES]
            if c:
                piece = pltpu.roll(piece, c, 1)
            band_ref[c * WIDTH : (c + 1) * WIDTH, d * LANES : (d + 1) * LANES] = piece.astype(BF16)
    bias_out[...] = column(0.5 * bias_ref[...])
    for tap in range(9):
        following_out[:, tap * WIDTH : (tap + 1) * WIDTH] = flip(following_ref[tap])
    for layer in range(LAYERS):
        for n in range(2):
            scales_out[2 * layer + n] = column(scales_ref[2 * layer + n : 2 * layer + n + 1])
        for n in range(3):
            qkv_out[layer, n * WIDTH : (n + 1) * WIDTH] = flip(
                qkv_ref[layer, :, n * WIDTH : (n + 1) * WIDTH]
            )
        out_w_out[layer] = flip(out_w_ref[layer])
        for n in range(FF // WIDTH):
            cut = slice(n * WIDTH, (n + 1) * WIDTH)
            up_w_out[layer, cut] = flip(0.5 * up_w_ref[layer, :, cut].astype(F32))
            down_w_out[layer, :, cut] = flip(down_w_ref[layer, cut])
    scales_out[2 * LAYERS] = column(closing_ref[...])
    turned = readout_ref[...].astype(F32).T
    readout_out[...] = jnp.concatenate(
        [turned, jnp.zeros((16 - OUT_FIELDS, WIDTH), F32)], axis=0
    ).astype(BF16)


def main_kernel(message_ref, *refs, pairs, lag):
    held_refs, refs = refs[: len(HELD)], refs[len(HELD) :]
    result_ref, first_ref, logit_ref, read_ref = refs[:4]
    local_refs, sems = refs[4:-1], refs[-1]
    copies = [
        pltpu.make_async_copy(held_refs[n], local_refs[n], sems.at[n]) for n in range(len(HELD))
    ]
    for copy in copies:
        copy.start()
    (
        band_ref, bias_ref, following_ref, scales_ref, qkv_ref, out_w_ref, up_w_ref, down_w_ref,
        readout_ref,
    ) = local_refs
    mem = lax.axis_index("mem")
    sp = lax.axis_index("sp")
    low = iota((WIDTH, LANES), 1) < 64

    rows = []
    for source, slot in ((0, 1), (0, 0), (1, 0), (1, 1)):
        block = message_ref[source * 8 : source * 8 + 8, slot * 16 : slot * 16 + 16, :]
        block = block.astype(F32).reshape(8, 2, 8, LANES)
        for r in range(2):
            rows.append(block[:, r].reshape(64, LANES))
    for p in range(CELL_PAIRS):
        q, c = p // COLUMNS, p % COLUMNS
        lane = c * SLOT + 12
        spread = jnp.concatenate(
            [
                jnp.broadcast_to(rows[2 + 2 * q + r][:, lane : lane + 1], (64, 64))
                for r in range(2)
            ],
            axis=1,
        )
        logit_ref[p] = spread * LOG2E
    taken = [row.astype(BF16) for row in rows]
    window = jnp.concatenate(
        [jnp.concatenate(taken[d : d + 6], axis=0) for d in range(3)], axis=1
    )
    chip = sp // 2
    block = (sp % 2) * lax.axis_size("mem") + mem
    top = jnp.where(low & (chip == 0), 0.0, 1.0)
    bottom = jnp.where(low | (chip < lax.axis_size("sp") // 2 - 1), 1.0, 0.0)
    left = jnp.where(block > 0, 1.0, 0.0)
    right = jnp.where(block < 2 * lax.axis_size("mem") - 1, 1.0, 0.0)
    copies[0].wait()
    copies[1].wait()
    bias = bias_ref[...]

    for start in range(0, WINDOW, 2):
        summed = lax.dot_general(
            band_ref[start * WIDTH : (start + 2) * WIDTH],
            window,
            NT,
            preferred_element_type=F32,
        )
        for n in range(2):
            c = start + n
            two = []
            for t, keep in enumerate((top, None, bottom)):
                part = gelu(
                    summed[n * WIDTH : (n + 1) * WIDTH, t * LANES : (t + 1) * LANES] + bias
                )
                if keep is not None:
                    part = part * keep
                if c in (0, WINDOW - 1):
                    part = part * (right if c else left)
                two.append(part)
            turned = [pltpu.roll(part, 64, 1) for part in two]
            for t in range(3):
                first_ref[2 * t, c] = two[t].astype(BF16)
            for t in range(2):
                first_ref[2 * t + 1, c] = jnp.where(low, turned[t], turned[t + 1]).astype(BF16)

    for copy in copies[2:]:
        copy.wait()
    key_mask = exact(
        iota((256, WIDTH), 0) // 64 == (iota((256, WIDTH), 1) // 16) % 4
    )
    value_mask = exact(iota((64, 256), 0) // 16 == iota((64, 256), 1) // 64)
    low_mask = exact(iota((WIDTH, LANES), 1) < 64)
    high_mask = exact(iota((WIDTH, LANES), 1) >= 64)
    scales = [scales_ref[n] for n in range(2 * LAYERS + 1)]

    def norm(stream, scale):
        parts = []
        for n in range(pairs):
            part = lanes_of(stream, n)
            centred = part - jnp.mean(part, 0, keepdims=True)
            variance = jnp.mean(centred * centred, 0, keepdims=True)
            parts.append((centred * lax.rsqrt(variance + EPS) * scale).astype(BF16))
        return jnp.concatenate(parts, axis=1)

    def lanes_of(value, n):
        return value[:, n * LANES : (n + 1) * LANES]

    groups = CELL_PAIRS // pairs
    streams = {}
    kept = {}

    def follow(group):
        taps = []
        for d in range(3):
            for e in range(3):
                parts = []
                for p in range(group * pairs, (group + 1) * pairs):
                    parts.append(first_ref[2 * (p // COLUMNS) + d, p % COLUMNS + e])
                taps.append(jnp.concatenate(parts, axis=1))
        stream = matmul(following_ref[...], jnp.concatenate(taps, axis=0))
        streams[group] = (stream + taps[4].astype(F32)).astype(BF16).astype(F32)

    def project(layer, group):
        normed = norm(streams[group], scales[2 * layer])
        kept[group, "triple"] = matmul(qkv_ref[layer], normed)

    def split(group, n):
        part = lanes_of(kept[group, "triple"], n)
        query = (part[:WIDTH] * (LOG2E / 4.0)).astype(BF16)
        cells = [query * low_mask, query * high_mask]
        zeros = jnp.zeros((64, LANES), BF16)
        query = jnp.concatenate(
            [
                jnp.concatenate([each for cell in cells for each in (cell[:64], zeros)], axis=0),
                jnp.concatenate([each for cell in cells for each in (zeros, cell[64:])], axis=0),
            ],
            axis=1,
        )
        key = part[WIDTH : 2 * WIDTH].T.astype(BF16)
        value = part[2 * WIDTH :]
        turned = pltpu.roll(value, 64, 1).astype(BF16)
        value = value.astype(BF16)
        values = [
            value * low_mask + turned * high_mask,
            turned * low_mask + value * high_mask,
        ]
        kept[group, n] = query, key, values

    def score(group, n):
        query, key, _ = kept[group, n]
        keys = jnp.concatenate(
            [
                jnp.concatenate([key[64 * r : 64 * r + 64]] * 4, axis=0) * key_mask
                for r in range(2)
            ],
            axis=1,
        )
        scores = matmul(keys, query)
        for half in range(2):
            kept[group, n, half] = lanes_of(scores, half)

    def soften(group, n, half):
        scores = kept[group, n, half].reshape(4, 64, LANES)
        scores = scores + logit_ref[group * pairs + n][None]
        raised = jnp.exp2(scores - jnp.max(scores, 1, keepdims=True))
        kept[group, n, half] = (
            raised.astype(BF16).reshape(256, LANES),
            1.0 / jnp.sum(raised, 1, keepdims=True),
        )

    def gather(group, n, half):
        raised, inverse = kept[group, n, half]
        spread = [
            jnp.concatenate([v[64 * half : 64 * half + 64]] * 2, axis=1) * value_mask
            for v in kept[group, n][2]
        ]
        found = matmul(jnp.concatenate(spread, axis=0), raised)
        picked = jnp.where(low[:64], found[:64], found[64:]).reshape(4, 16, LANES)
        kept[group, n, half] = (picked * inverse).reshape(64, LANES).astype(BF16)

    def attend(layer, group):
        attended = jnp.concatenate(
            [
                jnp.concatenate([kept[group, n, half] for half in range(2)], axis=0)
                for n in range(pairs)
            ],
            axis=1,
        )
        streams[group] = streams[group] + matmul(out_w_ref[layer], attended)

    def renorm(layer, group):
        kept[group, "normed"] = norm(streams[group], scales[2 * layer + 1])

    def widen(layer, group, q):
        cut = slice(q * WIDTH, (q + 1) * WIDTH)
        kept[group, "hidden", q] = matmul(up_w_ref[layer, cut], kept[group, "normed"])

    def bend(group, q):
        kept[group, "hidden", q] = gelu(kept[group, "hidden", q]).astype(BF16)

    def narrow(layer, group):
        hidden = jnp.concatenate(
            [kept[group, "hidden", q] for q in range(FF // WIDTH)], axis=0
        )
        streams[group] = streams[group] + matmul(down_w_ref[layer], hidden)

    def read(group):
        correction = matmul(readout_ref[...], norm(streams[group], scales[2 * LAYERS]))
        for n in range(pairs):
            for f in range(OUT_FIELDS):
                at = f * 16 + group * pairs + n
                read_ref[at : at + 1, :] = lanes_of(correction, n)[f : f + 1]

    issue = []
    slots = 2 * pairs
    for layer in range(LAYERS):
        for group in range(groups):
            base = (layer * groups + group) * slots

            def add(offset, step, *arguments, base=base):
                issue.append((base + offset, len(issue), step, arguments))

            if layer == 0:
                add(-2, follow, group)
            add(0, project, layer, group)
            at = 2
            for n in range(pairs):
                add(at + 2 * n, split, group, n)
                add(at + 2 * n + lag[0], score, group, n)
                for half in range(2):
                    k = at + 2 * n + half
                    add(k + lag[0] + lag[1], soften, group, n, half)
                    add(k + lag[0] + lag[1] + lag[2], gather, group, n, half)
            at = at + slots - 1 + sum(lag[:3]) + 1
            add(at, attend, layer, group)
            add(at + 1, renorm, layer, group)
            for q in range(4):
                add(at + 2 + q, widen, layer, group, q)
                add(at + 2 + q + lag[3], bend, group, q)
            at = at + 2 + 3 + lag[3] + 1
            add(at, narrow, layer, group)
            if layer == LAYERS - 1:
                add(at + 1, read, group)
    issue.sort(key=lambda entry: entry[:2])
    for _, _, step, arguments in issue:
        step(*arguments)

    turned = jnp.concatenate([read_ref[...], jnp.zeros((LANES - 32, LANES), F32)], axis=0).T
    result = turned[:64] + pltpu.roll(turned[64:], 32, 1)
    for s in range(2):
        result_ref[s * 8 : s * 8 + 8] = result.reshape(8, 8, LANES)


def unpack_kernel(got_ref, own_ref, out_ref):
    i = iota((32, LANES), 0)
    k = iota((32, LANES), 1)
    order = (k == (i % 8) * 16 + i // 8).astype(F32).astype(BF16)
    fields = matmul(order, own_ref[...])
    part = iota((8, LANES), 1) // COLUMNS
    odd = lax.axis_index("sp") % 2 == 1
    pieces = []
    for source in range(16):
        piece = got_ref[source]
        pieces.append(jnp.where(odd, pltpu.roll(piece, LANES - COLUMNS, 1), piece))
    for f in range(OUT_FIELDS):
        for r in range(2):
            n = 2 * f + r
            total = fields[n * 8 : n * 8 + 8]
            for source in range(16):
                shift = (COLUMNS * source - (r * 32 + f * 16)) % LANES
                piece = pieces[source]
                if shift:
                    piece = pltpu.roll(piece, shift, 1)
                total = total + jnp.where(part == source, piece, 0.0)
            out_ref[:, n, :] = total


HELD = (
    ((WINDOW * WIDTH, 3 * LANES), BF16),
    ((WIDTH, LANES), F32),
    ((WIDTH, 9 * WIDTH), BF16),
    ((2 * LAYERS + 1, WIDTH, LANES), F32),
    ((LAYERS, 3 * WIDTH, WIDTH), BF16),
    ((LAYERS, WIDTH, WIDTH), BF16),
    ((LAYERS, FF, WIDTH), BF16),
    ((LAYERS, WIDTH, FF), BF16),
    ((16, WIDTH), BF16),
)
IN_VMEM = pl.BlockSpec(memory_space=pltpu.VMEM)
IN_HBM = pl.BlockSpec(memory_space=pltpu.HBM)


def call(kernel, out_shape, args, limit, in_specs=None, scratch=()):
    return pl.pallas_call(
        kernel,
        out_shape=out_shape,
        in_specs=in_specs or [pl.BlockSpec()] * len(args),
        scratch_shapes=list(scratch),
        compiler_params=pltpu.CompilerParams(vmem_limit_bytes=limit * 1024 * 1024),
    )(*args)


def shape(dims, dtype):
    return jax.ShapeDtypeStruct(dims, dtype)


def in_hbm(value):
    return pltpu.with_memory_space_constraint(value, pltpu.HBM)


def main_call(arrived, prepared, **options):
    def main(*refs):
        main_kernel(*refs, **options)

    return call(
        main,
        shape((16, 8, LANES), F32),
        (arrived,) + tuple(in_hbm(each) for each in prepared),
        MAIN_LIMIT,
        [pl.BlockSpec()] + [IN_HBM] * len(HELD),
        [
            pltpu.VMEM((5, WINDOW, WIDTH, LANES), BF16),
            pltpu.VMEM((CELL_PAIRS, 64, LANES), F32),
            pltpu.VMEM((32, LANES), F32),
        ]
        + [pltpu.VMEM(*each) for each in HELD]
        + [pltpu.SemaphoreType.DMA((len(HELD),))],
    )


def shards(
    member_predictors,
    member_skill_logit,
    opening_filter,
    opening_bias,
    following_filter,
    layer_norm_scales,
    query_key_value_weight,
    attention_output_weight,
    upward_weight,
    downward_weight,
    closing_norm_scale,
    readout_weight,
):
    own = member_predictors.reshape(LANES, LANES)
    mems, sps = lax.axis_size("mem"), lax.axis_size("sp")
    swap = []
    for i in range(1, sps - 2, 2):
        swap += [(i, i + 1), (i + 1, i)]
    other = lax.ppermute(own, "sp", swap)
    message = call(
        pack_kernel,
        shape((16, 32, LANES), BF16),
        (other, in_hbm(own), in_hbm(member_skill_logit.reshape(16, LANES))),
        PACK_LIMIT,
        [pl.BlockSpec()] + [IN_HBM] * 2,
        (
            pltpu.VMEM((LANES, LANES), BF16),
            pltpu.VMEM((16, LANES), BF16),
            pltpu.SemaphoreType.DMA((2,)),
        ),
    )
    groups = [
        [m * sps + 2 * k + s for s in range(2) for m in range(mems)] for k in range(sps // 2)
    ]

    def exchange(value):
        return lax.all_to_all(
            value, ("mem", "sp"), 0, 0, tiled=True, axis_index_groups=groups
        )

    arrived = exchange(message)
    prepared = call(
        prepare_kernel,
        tuple(shape(*each) for each in HELD),
        (
            opening_filter,
            opening_bias.reshape(1, WIDTH),
            following_filter,
            layer_norm_scales.reshape(2 * LAYERS, WIDTH),
            closing_norm_scale.reshape(1, WIDTH),
            query_key_value_weight,
            attention_output_weight,
            upward_weight,
            downward_weight,
            readout_weight,
        ),
        60,
    )

    result = main_call(arrived, prepared, pairs=8, lag=(1, 2, 2, 1))
    got = exchange(result)
    output = call(unpack_kernel, shape((8, 4, LANES), F32), (got, own), UNPACK_LIMIT)
    return output.reshape(8, OUT_FIELDS, 2, LANES)


def solution(mesh):
    in_specs = (
        P("mem", None, "sp", None),
        P("mem", "sp", None),
        P(),
        P(),
        P(),
        P(),
        P(),
        P(),
        P(),
        P(),
        P(),
        P(),
    )
    out_specs = P("mem", None, "sp", None)
    return jax.shard_map(shards, mesh=mesh, in_specs=in_specs, out_specs=out_specs, check_vma=False)
```

```python
import math

import jax
import jax.numpy as jnp
from jax import lax
from jax.experimental import pallas as pl
from jax.experimental.pallas import tpu as pltpu
from jax.sharding import PartitionSpec as P

LAYERS = 2
WIDTH = 128
FF = 512
FIELDS = 8
OUT_FIELDS = 2
LANES = 128
SLOT = 16
COLUMNS = 8
WINDOW = COLUMNS + 2
CELL_PAIRS = 2 * COLUMNS
EPS = 1e-05
LOG2E = math.log2(math.e)
GELU_A = math.sqrt(2.0 / math.pi)
GELU_B = GELU_A * 0.044715

PACK_LIMIT = 8
MAIN_LIMIT = 48
UNPACK_LIMIT = 8

F32 = jnp.float32
BF16 = jnp.bfloat16
NT = (((1,), (1,)), ((), ()))


def iota(shape, dim):
    return lax.broadcasted_iota(jnp.int32, shape, dim)


def matmul(a, b):
    return jnp.dot(a, b, preferred_element_type=F32)


def exact(condition):
    return condition.astype(F32).astype(BF16)


def gelu(half):
    return half + half * jnp.tanh(half * (2.0 * GELU_A + 8.0 * GELU_B * (half * half)))


def pack(rows, logits, store):
    i = iota((LANES, LANES), 0)
    k = iota((LANES, LANES), 1)
    order = exact(k == (i % 8) * 16 + (i // 16) * 2 + (i // 8) % 2)
    c = iota((LANES, 2 * LANES), 0)
    lane = iota((LANES, 2 * LANES), 1)
    dest = lane // SLOT
    j = lane % SLOT
    pick = exact((c == COLUMNS * dest - 2 + j) & (j < 12))
    if logits is not None:
        li = iota((16, 16), 0)
        lk = iota((16, 16), 1)
        order_logit = exact(lk == (li % 8) * 2 + li // 8)
        stretch = exact((c == COLUMNS * dest + j) & (j < COLUMNS))
        logits = matmul(matmul(order_logit, logits).astype(BF16), stretch)
    spot = iota((16, LANES), 1) % SLOT == 12
    masks = [(iota((16, LANES), 1) // SLOT // (1 << bit)) % 2 == 0 for bit in range(3)]
    picked = matmul(matmul(order, rows).astype(BF16), pick)
    for q in range(2):
        cut = slice(q * LANES, (q + 1) * LANES)
        blocks = []
        for f in range(FIELDS):
            block = picked[f * 16 : f * 16 + 16, cut]
            if logits is not None:
                block = jnp.where(spot, pltpu.roll(logits[:, cut], 12 - f, 1), block)
            blocks.append(block)
        for bit in range(3):
            step = 1 << bit
            shift = SLOT * step
            for f in range(FIELDS):
                if f & step == 0:
                    first, other = blocks[f], blocks[f + step]
                    blocks[f] = jnp.where(masks[bit], first, pltpu.roll(other, shift, 1))
                    blocks[f + step] = jnp.where(
                        masks[bit], pltpu.roll(first, LANES - shift, 1), other
                    )
        for n in range(8):
            store(8 * q + n, blocks[n].astype(BF16))


def pack_own_kernel(own_ref, logit_ref, out_ref):
    def store(n, value):
        out_ref[n] = value

    pack(own_ref[...], logit_ref[...], store)


def pack_other_kernel(other_ref, part_ref, out_ref):
    out_ref[:, :16, :] = part_ref[...]

    def store(n, value):
        out_ref[n, 16:, :] = value

    pack(other_ref[...], None, store)


def prepare_kernel(
    opening_ref, bias_ref, following_ref, scales_ref, closing_ref, qkv_ref, out_w_ref, up_w_ref,
    down_w_ref, readout_ref,
    band_ref, bias_out, following_out, scales_out, qkv_out, out_w_out, up_w_out, down_w_out,
    readout_out,
):
    def flip(value):
        return value.astype(F32).T.astype(BF16)

    def column(row):
        return jnp.broadcast_to(row, (LANES, LANES)).T

    t = iota((72, 3 * LANES), 0)
    lane = iota((72, 3 * LANES), 1)
    tap = t // 8
    place = exact(
        (lane // LANES == tap // 3)
        & ((lane % LANES) // SLOT == t % 8)
        & (lane % SLOT == tap % 3)
    )
    flat = opening_ref[...].astype(F32).reshape(72, WIDTH)
    base = 0.5 * matmul(flat.T.astype(BF16), place)
    for c in range(WINDOW):
        for d in range(3):
            piece = base[:, d * LANES : (d + 1) * LANES]
            if c:
                piece = pltpu.roll(piece, c, 1)
            band_ref[c * WIDTH : (c + 1) * WIDTH, d * LANES : (d + 1) * LANES] = piece.astype(BF16)
    bias_out[...] = column(0.5 * bias_ref[...])
    for tap in range(9):
        following_out[:, tap * WIDTH : (tap + 1) * WIDTH] = flip(following_ref[tap])
    for layer in range(LAYERS):
        for n in range(2):
            scales_out[2 * layer + n] = column(scales_ref[2 * layer + n : 2 * layer + n + 1])
        for n in range(3):
            qkv_out[layer, n * WIDTH : (n + 1) * WIDTH] = flip(
                qkv_ref[layer, :, n * WIDTH : (n + 1) * WIDTH]
            )
        out_w_out[layer] = flip(out_w_ref[layer])
        for n in range(FF // WIDTH):
            cut = slice(n * WIDTH, (n + 1) * WIDTH)
            up_w_out[layer, cut] = flip(0.5 * up_w_ref[layer, :, cut].astype(F32))
            down_w_out[layer, :, cut] = flip(down_w_ref[layer, cut])
    scales_out[2 * LAYERS] = column(closing_ref[...])
    turned = readout_ref[...].astype(F32)
    readout_out[...] = jnp.concatenate(
        [turned, jnp.zeros((16 - OUT_FIELDS, WIDTH), F32)], axis=0
    ).astype(BF16)


def main_kernel(message_ref, *refs, pairs, lag):
    held_refs, refs = refs[: len(HELD)], refs[len(HELD) :]
    result_ref, first_ref, logit_ref, read_ref = refs[:4]
    local_refs, sems = refs[4:-1], refs[-1]
    copies = [
        pltpu.make_async_copy(held_refs[n], local_refs[n], sems.at[n]) for n in range(len(HELD))
    ]
    for copy in copies:
        copy.start()
    (
        band_ref, bias_ref, following_ref, scales_ref, qkv_ref, out_w_ref, up_w_ref, down_w_ref,
        readout_ref,
    ) = local_refs
    mem = lax.axis_index("mem")
    sp = lax.axis_index("sp")
    low = iota((WIDTH, LANES), 1) < 64

    rows = []
    for source, slot in ((0, 1), (0, 0), (1, 0), (1, 1)):
        block = message_ref[source * 8 : source * 8 + 8, slot * 16 : slot * 16 + 16, :]
        block = block.astype(F32).reshape(8, 2, 8, LANES)
        for r in range(2):
            rows.append(block[:, r].reshape(64, LANES))
    for p in range(CELL_PAIRS):
        q, c = p // COLUMNS, p % COLUMNS
        lane = c * SLOT + 12
        spread = jnp.concatenate(
            [
                jnp.broadcast_to(rows[2 + 2 * q + r][:, lane : lane + 1], (64, 64))
                for r in range(2)
            ],
            axis=1,
        )
        logit_ref[p] = spread * LOG2E
    taken = [row.astype(BF16) for row in rows]
    window = jnp.concatenate(
        [jnp.concatenate(taken[d : d + 6], axis=0) for d in range(3)], axis=1
    )
    chip = sp // 2
    block = (sp % 2) * lax.axis_size("mem") + mem
    top = jnp.where(low & (chip == 0), 0.0, 1.0)
    bottom = jnp.where(low | (chip < lax.axis_size("sp") // 2 - 1), 1.0, 0.0)
    left = jnp.where(block > 0, 1.0, 0.0)
    right = jnp.where(block < 2 * lax.axis_size("mem") - 1, 1.0, 0.0)
    for copy in copies:
        copy.wait()
    bias = bias_ref[...]

    for start in range(0, WINDOW, 2):
        summed = lax.dot_general(
            band_ref[start * WIDTH : (start + 2) * WIDTH],
            window,
            NT,
            preferred_element_type=F32,
        )
        for n in range(2):
            c = start + n
            two = []
            for t, keep in enumerate((top, None, bottom)):
                part = gelu(
                    summed[n * WIDTH : (n + 1) * WIDTH, t * LANES : (t + 1) * LANES] + bias
                )
                if keep is not None:
                    part = part * keep
                if c in (0, WINDOW - 1):
                    part = part * (right if c else left)
                two.append(part)
            turned = [pltpu.roll(part, 64, 1) for part in two]
            for t in range(3):
                first_ref[2 * t, c] = two[t].astype(BF16)
            for t in range(2):
                first_ref[2 * t + 1, c] = jnp.where(low, turned[t], turned[t + 1]).astype(BF16)

    key_mask = exact(
        iota((256, WIDTH), 0) // 64 == (iota((256, WIDTH), 1) // 16) % 4
    )
    value_mask = exact(iota((64, 256), 0) // 16 == iota((64, 256), 1) // 64)
    low_mask = exact(iota((WIDTH, LANES), 1) < 64)
    high_mask = exact(iota((WIDTH, LANES), 1) >= 64)
    scales = [scales_ref[n] for n in range(2 * LAYERS + 1)]

    def norm(stream, scale):
        parts = []
        for n in range(pairs):
            part = lanes_of(stream, n)
            centred = part - jnp.mean(part, 0, keepdims=True)
            variance = jnp.mean(centred * centred, 0, keepdims=True)
            parts.append((centred * lax.rsqrt(variance + EPS) * scale).astype(BF16))
        return jnp.concatenate(parts, axis=1)

    def lanes_of(value, n):
        return value[:, n * LANES : (n + 1) * LANES]

    groups = CELL_PAIRS // pairs
    streams = {}
    kept = {}

    def follow(group):
        taps = []
        for d in range(3):
            for e in range(3):
                parts = []
                for p in range(group * pairs, (group + 1) * pairs):
                    parts.append(first_ref[2 * (p // COLUMNS) + d, p % COLUMNS + e])
                taps.append(jnp.concatenate(parts, axis=1))
        stream = matmul(following_ref[...], jnp.concatenate(taps, axis=0))
        streams[group] = (stream + taps[4].astype(F32)).astype(BF16).astype(F32)

    def project(layer, group):
        normed = norm(streams[group], scales[2 * layer])
        kept[group, "triple"] = matmul(qkv_ref[layer], normed)

    def split(group, n):
        part = lanes_of(kept[group, "triple"], n)
        query = (part[:WIDTH] * (LOG2E / 4.0)).astype(BF16)
        cells = [query * low_mask, query * high_mask]
        zeros = jnp.zeros((64, LANES), BF16)
        query = jnp.concatenate(
            [
                jnp.concatenate([each for cell in cells for each in (cell[:64], zeros)], axis=0),
                jnp.concatenate([each for cell in cells for each in (zeros, cell[64:])], axis=0),
            ],
            axis=1,
        )
        key = part[WIDTH : 2 * WIDTH].T.astype(BF16)
        value = part[2 * WIDTH :]
        turned = pltpu.roll(value, 64, 1).astype(BF16)
        value = value.astype(BF16)
        values = [
            value * low_mask + turned * high_mask,
            turned * low_mask + value * high_mask,
        ]
        kept[group, n] = query, key, values

    def score(group, n):
        query, key, _ = kept[group, n]
        keys = jnp.concatenate(
            [
                jnp.concatenate([key[64 * r : 64 * r + 64]] * 4, axis=0) * key_mask
                for r in range(2)
            ],
            axis=1,
        )
        scores = matmul(keys, query)
        for half in range(2):
            kept[group, n, half] = lanes_of(scores, half)

    def soften(group, n, half):
        scores = kept[group, n, half].reshape(4, 64, LANES)
        scores = scores + logit_ref[group * pairs + n][None]
        raised = jnp.exp2(scores - jnp.max(scores, 1, keepdims=True))
        kept[group, n, half] = (
            raised.astype(BF16).reshape(256, LANES),
            1.0 / jnp.sum(raised, 1, keepdims=True),
        )

    def gather(group, n, half):
        raised, inverse = kept[group, n, half]
        spread = [
            jnp.concatenate([v[64 * half : 64 * half + 64]] * 2, axis=1) * value_mask
            for v in kept[group, n][2]
        ]
        found = matmul(jnp.concatenate(spread, axis=0), raised)
        picked = jnp.where(low[:64], found[:64], found[64:]).reshape(4, 16, LANES)
        kept[group, n, half] = (picked * inverse).reshape(64, LANES).astype(BF16)

    def attend(layer, group):
        attended = jnp.concatenate(
            [
                jnp.concatenate([kept[group, n, half] for half in range(2)], axis=0)
                for n in range(pairs)
            ],
            axis=1,
        )
        streams[group] = streams[group] + matmul(out_w_ref[layer], attended)

    def renorm(layer, group):
        kept[group, "normed"] = norm(streams[group], scales[2 * layer + 1])

    def widen(layer, group, q):
        cut = slice(q * WIDTH, (q + 1) * WIDTH)
        kept[group, "hidden", q] = matmul(up_w_ref[layer, cut], kept[group, "normed"])

    def bend(group, q):
        kept[group, "hidden", q] = gelu(kept[group, "hidden", q]).astype(BF16)

    def narrow(layer, group):
        hidden = jnp.concatenate(
            [kept[group, "hidden", q] for q in range(FF // WIDTH)], axis=0
        )
        streams[group] = streams[group] + matmul(down_w_ref[layer], hidden)

    def read(group):
        correction = matmul(readout_ref[...], norm(streams[group], scales[2 * LAYERS]))
        for n in range(pairs):
            for f in range(OUT_FIELDS):
                at = f * 16 + group * pairs + n
                read_ref[at : at + 1, :] = lanes_of(correction, n)[f : f + 1]

    issue = []
    slots = 2 * pairs
    for layer in range(LAYERS):
        for group in range(groups):
            base = (layer * groups + group) * slots

            def add(offset, step, *arguments, base=base):
                issue.append((base + offset, len(issue), step, arguments))

            if layer == 0:
                add(-2, follow, group)
            add(0, project, layer, group)
            at = 2
            for n in range(pairs):
                add(at + 2 * n, split, group, n)
                add(at + 2 * n + lag[0], score, group, n)
                for half in range(2):
                    k = at + 2 * n + half
                    add(k + lag[0] + lag[1], soften, group, n, half)
                    add(k + lag[0] + lag[1] + lag[2], gather, group, n, half)
            at = at + slots - 1 + sum(lag[:3]) + 1
            add(at, attend, layer, group)
            add(at + 1, renorm, layer, group)
            for q in range(4):
                add(at + 2 + q, widen, layer, group, q)
                add(at + 2 + q + lag[3], bend, group, q)
            at = at + 2 + 3 + lag[3] + 1
            add(at, narrow, layer, group)
            if layer == LAYERS - 1:
                add(at + 1, read, group)
    issue.sort(key=lambda entry: entry[:2])
    for _, _, step, arguments in issue:
        step(*arguments)

    turned = jnp.concatenate([read_ref[...], jnp.zeros((LANES - 32, LANES), F32)], axis=0).T
    result = turned[:64] + pltpu.roll(turned[64:], 32, 1)
    for s in range(2):
        result_ref[s * 8 : s * 8 + 8] = result.reshape(8, 8, LANES)


def unpack_kernel(got_ref, own_ref, out_ref):
    i = iota((32, LANES), 0)
    k = iota((32, LANES), 1)
    order = (k == (i % 8) * 16 + i // 8).astype(F32).astype(BF16)
    fields = matmul(order, own_ref[...])
    part = iota((8, LANES), 1) // COLUMNS
    odd = lax.axis_index("sp") % 2 == 1
    pieces = []
    for source in range(16):
        piece = got_ref[source]
        pieces.append(jnp.where(odd, pltpu.roll(piece, LANES - COLUMNS, 1), piece))
    for f in range(OUT_FIELDS):
        for r in range(2):
            n = 2 * f + r
            total = fields[n * 8 : n * 8 + 8]
            for source in range(16):
                shift = (COLUMNS * source - (r * 32 + f * 16)) % LANES
                piece = pieces[source]
                if shift:
                    piece = pltpu.roll(piece, shift, 1)
                total = total + jnp.where(part == source, piece, 0.0)
            out_ref[:, n, :] = total


HELD = (
    ((WINDOW * WIDTH, 3 * LANES), BF16),
    ((WIDTH, LANES), F32),
    ((WIDTH, 9 * WIDTH), BF16),
    ((2 * LAYERS + 1, WIDTH, LANES), F32),
    ((LAYERS, 3 * WIDTH, WIDTH), BF16),
    ((LAYERS, WIDTH, WIDTH), BF16),
    ((LAYERS, FF, WIDTH), BF16),
    ((LAYERS, WIDTH, FF), BF16),
    ((16, WIDTH), BF16),
)
IN_VMEM = pl.BlockSpec(memory_space=pltpu.VMEM)
IN_HBM = pl.BlockSpec(memory_space=pltpu.HBM)


def call(kernel, out_shape, args, limit, in_specs=None, scratch=()):
    return pl.pallas_call(
        kernel,
        out_shape=out_shape,
        in_specs=in_specs or [pl.BlockSpec()] * len(args),
        scratch_shapes=list(scratch),
        compiler_params=pltpu.CompilerParams(vmem_limit_bytes=limit * 1024 * 1024),
    )(*args)


def shape(dims, dtype):
    return jax.ShapeDtypeStruct(dims, dtype)


def in_hbm(value):
    return pltpu.with_memory_space_constraint(value, pltpu.HBM)


def main_call(arrived, prepared, **options):
    def main(*refs):
        main_kernel(*refs, **options)

    return call(
        main,
        shape((16, 8, LANES), F32),
        (arrived,) + tuple(in_hbm(each) for each in prepared),
        MAIN_LIMIT,
        [pl.BlockSpec()] + [IN_HBM] * len(HELD),
        [
            pltpu.VMEM((5, WINDOW, WIDTH, LANES), BF16),
            pltpu.VMEM((CELL_PAIRS, 64, LANES), F32),
            pltpu.VMEM((32, LANES), F32),
        ]
        + [pltpu.VMEM(*each) for each in HELD]
        + [pltpu.SemaphoreType.DMA((WINDOW // 2 + len(HELD) - 1,))],
    )


def shards(
    member_predictors,
    member_skill_logit,
    opening_filter,
    opening_bias,
    following_filter,
    layer_norm_scales,
    query_key_value_weight,
    attention_output_weight,
    upward_weight,
    downward_weight,
    closing_norm_scale,
    readout_weight,
):
    own = member_predictors.reshape(LANES, LANES)
    mems, sps = lax.axis_size("mem"), lax.axis_size("sp")
    swap = []
    for i in range(1, sps - 2, 2):
        swap += [(i, i + 1), (i + 1, i)]
    other = lax.ppermute(own, "sp", swap)
    part = call(
        pack_own_kernel,
        shape((16, 16, LANES), BF16),
        (in_hbm(own), in_hbm(member_skill_logit.reshape(16, LANES))),
        PACK_LIMIT,
    )
    message = call(pack_other_kernel, shape((16, 32, LANES), BF16), (other, part), PACK_LIMIT)
    groups = [
        [m * sps + 2 * k + s for s in range(2) for m in range(mems)] for k in range(sps // 2)
    ]

    def exchange(value):
        return lax.all_to_all(
            value, ("mem", "sp"), 0, 0, tiled=True, axis_index_groups=groups
        )

    arrived = exchange(message)
    prepared = call(
        prepare_kernel,
        tuple(shape(*each) for each in HELD),
        (
            opening_filter,
            opening_bias.reshape(1, WIDTH),
            following_filter,
            layer_norm_scales.reshape(2 * LAYERS, WIDTH),
            closing_norm_scale.reshape(1, WIDTH),
            query_key_value_weight,
            attention_output_weight,
            upward_weight,
            downward_weight,
            readout_weight.T,
        ),
        60,
    )

    result = main_call(arrived, prepared, pairs=8, lag=(1, 1, 2, 1))
    got = exchange(result)
    output = call(unpack_kernel, shape((8, 4, LANES), F32), (got, own), UNPACK_LIMIT)
    return output.reshape(8, OUT_FIELDS, 2, LANES)


def solution(mesh):
    in_specs = (
        P("mem", None, "sp", None),
        P("mem", "sp", None),
        P(),
        P(),
        P(),
        P(),
        P(),
        P(),
        P(),
        P(),
        P(),
        P(),
    )
    out_specs = P("mem", None, "sp", None)
    return jax.shard_map(shards, mesh=mesh, in_specs=in_specs, out_specs=out_specs, check_vma=False)
```

```python
import math

import jax
import jax.numpy as jnp
from jax import lax
from jax.experimental import pallas as pl
from jax.experimental.pallas import tpu as pltpu
from jax.sharding import PartitionSpec as P

LAYERS = 2
WIDTH = 128
FF = 512
FIELDS = 8
OUT_FIELDS = 2
LANES = 128
SLOT = 16
COLUMNS = 8
WINDOW = COLUMNS + 2
CELL_PAIRS = 2 * COLUMNS
EPS = 1e-05
LOG2E = math.log2(math.e)
GELU_A = math.sqrt(2.0 / math.pi)
GELU_B = GELU_A * 0.044715

PACK_LIMIT = 8
MAIN_LIMIT = 40
PREPARE_LIMIT = 24
UNPACK_LIMIT = 8

F32 = jnp.float32
BF16 = jnp.bfloat16
NT = (((1,), (1,)), ((), ()))


def iota(shape, dim):
    return lax.broadcasted_iota(jnp.int32, shape, dim)


def matmul(a, b):
    return jnp.dot(a, b, preferred_element_type=F32)


def exact(condition):
    return condition.astype(F32).astype(BF16)


def gelu(half):
    return half + half * jnp.tanh(half * (2.0 * GELU_A + 8.0 * GELU_B * (half * half)))


def pack(rows, logits, store):
    i = iota((LANES, LANES), 0)
    k = iota((LANES, LANES), 1)
    order = exact(k == (i % 8) * 16 + (i // 16) * 2 + (i // 8) % 2)
    c = iota((LANES, 2 * LANES), 0)
    lane = iota((LANES, 2 * LANES), 1)
    dest = lane // SLOT
    j = lane % SLOT
    pick = exact((c == COLUMNS * dest - 2 + j) & (j < 12))
    if logits is not None:
        li = iota((16, 16), 0)
        lk = iota((16, 16), 1)
        order_logit = exact(lk == (li % 8) * 2 + li // 8)
        stretch = exact((c == COLUMNS * dest + j) & (j < COLUMNS))
        logits = matmul(matmul(order_logit, logits).astype(BF16), stretch)
    spot = iota((16, LANES), 1) % SLOT == 12
    masks = [(iota((16, LANES), 1) // SLOT // (1 << bit)) % 2 == 0 for bit in range(3)]
    picked = matmul(matmul(order, rows).astype(BF16), pick)
    for q in range(2):
        cut = slice(q * LANES, (q + 1) * LANES)
        blocks = []
        for f in range(FIELDS):
            block = picked[f * 16 : f * 16 + 16, cut]
            if logits is not None:
                block = jnp.where(spot, pltpu.roll(logits[:, cut], 12 - f, 1), block)
            blocks.append(block)
        for bit in range(3):
            step = 1 << bit
            shift = SLOT * step
            for f in range(FIELDS):
                if f & step == 0:
                    first, other = blocks[f], blocks[f + step]
                    blocks[f] = jnp.where(masks[bit], first, pltpu.roll(other, shift, 1))
                    blocks[f + step] = jnp.where(
                        masks[bit], pltpu.roll(first, LANES - shift, 1), other
                    )
        for n in range(8):
            store(8 * q + n, blocks[n].astype(BF16))


def pack_own_kernel(own_ref, logit_ref, out_ref):
    def store(n, value):
        out_ref[n] = value

    pack(own_ref[...], logit_ref[...], store)


def pack_other_kernel(other_ref, part_ref, out_ref):
    out_ref[:, :16, :] = part_ref[...]

    def store(n, value):
        out_ref[n, 16:, :] = value

    pack(other_ref[...], None, store)


def prepare_kernel(
    opening_ref, bias_ref, following_ref, scales_ref, closing_ref, qkv_ref, out_w_ref, up_w_ref,
    down_w_ref, readout_ref,
    band_ref, bias_out, following_out, scales_out, qkv_out, out_w_out, up_w_out, down_w_out,
    readout_out,
):
    def flip(value):
        return value.astype(F32).T.astype(BF16)

    def column(row):
        return jnp.broadcast_to(row, (LANES, LANES)).T

    t = iota((72, 3 * LANES), 0)
    lane = iota((72, 3 * LANES), 1)
    tap = t // 8
    place = exact(
        (lane // LANES == tap // 3)
        & ((lane % LANES) // SLOT == t % 8)
        & (lane % SLOT == tap % 3)
    )
    flat = opening_ref[...].astype(F32).reshape(72, WIDTH)
    base = 0.5 * matmul(flat.T.astype(BF16), place)
    for c in range(WINDOW):
        for d in range(3):
            piece = base[:, d * LANES : (d + 1) * LANES]
            if c:
                piece = pltpu.roll(piece, c, 1)
            band_ref[c * WIDTH : (c + 1) * WIDTH, d * LANES : (d + 1) * LANES] = piece.astype(BF16)
    bias_out[...] = column(0.5 * bias_ref[...])
    for tap in range(9):
        following_out[:, tap * WIDTH : (tap + 1) * WIDTH] = flip(following_ref[tap])
    for layer in range(LAYERS):
        for n in range(2):
            scales_out[2 * layer + n] = column(scales_ref[2 * layer + n : 2 * layer + n + 1])
        for n in range(3):
            qkv_out[layer, n * WIDTH : (n + 1) * WIDTH] = flip(
                qkv_ref[layer, :, n * WIDTH : (n + 1) * WIDTH]
            )
        out_w_out[layer] = flip(out_w_ref[layer])
        for n in range(FF // WIDTH):
            cut = slice(n * WIDTH, (n + 1) * WIDTH)
            up_w_out[layer, cut] = flip(0.5 * up_w_ref[layer, :, cut].astype(F32))
            down_w_out[layer, :, cut] = flip(down_w_ref[layer, cut])
    scales_out[2 * LAYERS] = column(closing_ref[...])
    turned = readout_ref[...].astype(F32)
    readout_out[...] = jnp.concatenate(
        [turned, jnp.zeros((16 - OUT_FIELDS, WIDTH), F32)], axis=0
    ).astype(BF16)


def main_kernel(message_ref, *refs, pairs, lag):
    held_refs, refs = refs[: len(HELD)], refs[len(HELD) :]
    result_ref, first_ref, logit_ref, read_ref = refs
    (
        band_ref, bias_ref, following_ref, scales_ref, qkv_ref, out_w_ref, up_w_ref, down_w_ref,
        readout_ref,
    ) = held_refs
    mem = lax.axis_index("mem")
    sp = lax.axis_index("sp")
    low = iota((WIDTH, LANES), 1) < 64

    rows = []
    for source, slot in ((0, 1), (0, 0), (1, 0), (1, 1)):
        block = message_ref[source * 8 : source * 8 + 8, slot * 16 : slot * 16 + 16, :]
        block = block.astype(F32).reshape(8, 2, 8, LANES)
        for r in range(2):
            rows.append(block[:, r].reshape(64, LANES))
    for p in range(CELL_PAIRS):
        q, c = p // COLUMNS, p % COLUMNS
        lane = c * SLOT + 12
        spread = jnp.concatenate(
            [
                jnp.broadcast_to(rows[2 + 2 * q + r][:, lane : lane + 1], (64, 64))
                for r in range(2)
            ],
            axis=1,
        )
        logit_ref[p] = spread * LOG2E
    taken = [row.astype(BF16) for row in rows]
    window = jnp.concatenate(
        [jnp.concatenate(taken[d : d + 6], axis=0) for d in range(3)], axis=1
    )
    chip = sp // 2
    block = (sp % 2) * lax.axis_size("mem") + mem
    top = jnp.where(low & (chip == 0), 0.0, 1.0)
    bottom = jnp.where(low | (chip < lax.axis_size("sp") // 2 - 1), 1.0, 0.0)
    left = jnp.where(block > 0, 1.0, 0.0)
    right = jnp.where(block < 2 * lax.axis_size("mem") - 1, 1.0, 0.0)
    bias = bias_ref[...]

    for start in range(0, WINDOW, 2):
        summed = lax.dot_general(
            band_ref[start * WIDTH : (start + 2) * WIDTH],
            window,
            NT,
            preferred_element_type=F32,
        )
        for n in range(2):
            c = start + n
            two = []
            for t, keep in enumerate((top, None, bottom)):
                part = gelu(
                    summed[n * WIDTH : (n + 1) * WIDTH, t * LANES : (t + 1) * LANES] + bias
                )
                if keep is not None:
                    part = part * keep
                if c in (0, WINDOW - 1):
                    part = part * (right if c else left)
                two.append(part)
            turned = [pltpu.roll(part, 64, 1) for part in two]
            for t in range(3):
                first_ref[2 * t, c] = two[t].astype(BF16)
            for t in range(2):
                first_ref[2 * t + 1, c] = jnp.where(low, turned[t], turned[t + 1]).astype(BF16)

    key_mask = exact(
        iota((256, WIDTH), 0) // 64 == (iota((256, WIDTH), 1) // 16) % 4
    )
    value_mask = exact(iota((64, 256), 0) // 16 == iota((64, 256), 1) // 64)
    low_mask = exact(iota((WIDTH, LANES), 1) < 64)
    high_mask = exact(iota((WIDTH, LANES), 1) >= 64)
    scales = [scales_ref[n] for n in range(2 * LAYERS + 1)]

    def norm(stream, scale):
        parts = []
        for n in range(pairs):
            part = lanes_of(stream, n)
            centred = part - jnp.mean(part, 0, keepdims=True)
            variance = jnp.mean(centred * centred, 0, keepdims=True)
            parts.append((centred * lax.rsqrt(variance + EPS) * scale).astype(BF16))
        return jnp.concatenate(parts, axis=1)

    def lanes_of(value, n):
        return value[:, n * LANES : (n + 1) * LANES]

    groups = CELL_PAIRS // pairs
    streams = {}
    kept = {}

    def follow(group):
        taps = []
        for d in range(3):
            for e in range(3):
                parts = []
                for p in range(group * pairs, (group + 1) * pairs):
                    parts.append(first_ref[2 * (p // COLUMNS) + d, p % COLUMNS + e])
                taps.append(jnp.concatenate(parts, axis=1))
        stream = matmul(following_ref[...], jnp.concatenate(taps, axis=0))
        streams[group] = (stream + taps[4].astype(F32)).astype(BF16).astype(F32)

    def project(layer, group):
        normed = norm(streams[group], scales[2 * layer])
        kept[group, "triple"] = matmul(qkv_ref[layer], normed)

    def split(group, n):
        part = lanes_of(kept[group, "triple"], n)
        query = (part[:WIDTH] * (LOG2E / 4.0)).astype(BF16)
        cells = [query * low_mask, query * high_mask]
        zeros = jnp.zeros((64, LANES), BF16)
        query = jnp.concatenate(
            [
                jnp.concatenate([each for cell in cells for each in (cell[:64], zeros)], axis=0),
                jnp.concatenate([each for cell in cells for each in (zeros, cell[64:])], axis=0),
            ],
            axis=1,
        )
        key = part[WIDTH : 2 * WIDTH].T.astype(BF16)
        value = part[2 * WIDTH :]
        turned = pltpu.roll(value, 64, 1).astype(BF16)
        value = value.astype(BF16)
        values = [
            value * low_mask + turned * high_mask,
            turned * low_mask + value * high_mask,
        ]
        kept[group, n] = query, key, values

    def score(group, n):
        query, key, _ = kept[group, n]
        keys = jnp.concatenate(
            [
                jnp.concatenate([key[64 * r : 64 * r + 64]] * 4, axis=0) * key_mask
                for r in range(2)
            ],
            axis=1,
        )
        scores = matmul(keys, query)
        for half in range(2):
            kept[group, n, half] = lanes_of(scores, half)

    def soften(group, n, half):
        scores = kept[group, n, half].reshape(4, 64, LANES)
        scores = scores + logit_ref[group * pairs + n][None]
        raised = jnp.exp2(scores - jnp.max(scores, 1, keepdims=True))
        kept[group, n, half] = (
            raised.astype(BF16).reshape(256, LANES),
            1.0 / jnp.sum(raised, 1, keepdims=True),
        )

    def gather(group, n, half):
        raised, inverse = kept[group, n, half]
        spread = [
            jnp.concatenate([v[64 * half : 64 * half + 64]] * 2, axis=1) * value_mask
            for v in kept[group, n][2]
        ]
        found = matmul(jnp.concatenate(spread, axis=0), raised)
        picked = jnp.where(low[:64], found[:64], found[64:]).reshape(4, 16, LANES)
        kept[group, n, half] = (picked * inverse).reshape(64, LANES).astype(BF16)

    def attend(layer, group):
        attended = jnp.concatenate(
            [
                jnp.concatenate([kept[group, n, half] for half in range(2)], axis=0)
                for n in range(pairs)
            ],
            axis=1,
        )
        streams[group] = streams[group] + matmul(out_w_ref[layer], attended)

    def renorm(layer, group):
        kept[group, "normed"] = norm(streams[group], scales[2 * layer + 1])

    def widen(layer, group, q):
        cut = slice(q * WIDTH, (q + 1) * WIDTH)
        kept[group, "hidden", q] = matmul(up_w_ref[layer, cut], kept[group, "normed"])

    def bend(group, q):
        kept[group, "hidden", q] = gelu(kept[group, "hidden", q]).astype(BF16)

    def narrow(layer, group):
        hidden = jnp.concatenate(
            [kept[group, "hidden", q] for q in range(FF // WIDTH)], axis=0
        )
        streams[group] = streams[group] + matmul(down_w_ref[layer], hidden)

    def read(group):
        correction = matmul(readout_ref[...], norm(streams[group], scales[2 * LAYERS]))
        for n in range(pairs):
            for f in range(OUT_FIELDS):
                at = f * 16 + group * pairs + n
                read_ref[at : at + 1, :] = lanes_of(correction, n)[f : f + 1]

    issue = []
    slots = 2 * pairs
    for layer in range(LAYERS):
        for group in range(groups):
            base = (layer * groups + group) * slots

            def add(offset, step, *arguments, base=base):
                issue.append((base + offset, len(issue), step, arguments))

            if layer == 0:
                add(-2, follow, group)
            add(0, project, layer, group)
            at = 2
            for n in range(pairs):
                add(at + 2 * n, split, group, n)
                add(at + 2 * n + lag[0], score, group, n)
                for half in range(2):
                    k = at + 2 * n + half
                    add(k + lag[0] + lag[1], soften, group, n, half)
                    add(k + lag[0] + lag[1] + lag[2], gather, group, n, half)
            at = at + slots - 1 + sum(lag[:3]) + 1
            add(at, attend, layer, group)
            add(at + 1, renorm, layer, group)
            for q in range(4):
                add(at + 2 + q, widen, layer, group, q)
                add(at + 2 + q + lag[3], bend, group, q)
            at = at + 2 + 3 + lag[3] + 1
            add(at, narrow, layer, group)
            if layer == LAYERS - 1:
                add(at + 1, read, group)
    issue.sort(key=lambda entry: entry[:2])
    for _, _, step, arguments in issue:
        step(*arguments)

    turned = jnp.concatenate([read_ref[...], jnp.zeros((LANES - 32, LANES), F32)], axis=0).T
    result = turned[:64] + pltpu.roll(turned[64:], 32, 1)
    for s in range(2):
        result_ref[s * 8 : s * 8 + 8] = result.reshape(8, 8, LANES)


def unpack_kernel(got_ref, own_ref, out_ref):
    i = iota((32, LANES), 0)
    k = iota((32, LANES), 1)
    order = (k == (i % 8) * 16 + i // 8).astype(F32).astype(BF16)
    fields = matmul(order, own_ref[...])
    part = iota((8, LANES), 1) // COLUMNS
    odd = lax.axis_index("sp") % 2 == 1
    pieces = []
    for source in range(16):
        piece = got_ref[source]
        pieces.append(jnp.where(odd, pltpu.roll(piece, LANES - COLUMNS, 1), piece))
    for f in range(OUT_FIELDS):
        for r in range(2):
            n = 2 * f + r
            total = fields[n * 8 : n * 8 + 8]
            for source in range(16):
                shift = (COLUMNS * source - (r * 32 + f * 16)) % LANES
                piece = pieces[source]
                if shift:
                    piece = pltpu.roll(piece, shift, 1)
                total = total + jnp.where(part == source, piece, 0.0)
            out_ref[:, n, :] = total


HELD = (
    ((WINDOW * WIDTH, 3 * LANES), BF16),
    ((WIDTH, LANES), F32),
    ((WIDTH, 9 * WIDTH), BF16),
    ((2 * LAYERS + 1, WIDTH, LANES), F32),
    ((LAYERS, 3 * WIDTH, WIDTH), BF16),
    ((LAYERS, WIDTH, WIDTH), BF16),
    ((LAYERS, FF, WIDTH), BF16),
    ((LAYERS, WIDTH, FF), BF16),
    ((16, WIDTH), BF16),
)
IN_VMEM = pl.BlockSpec(memory_space=pltpu.VMEM)
IN_HBM = pl.BlockSpec(memory_space=pltpu.HBM)


def call(kernel, out_shape, args, limit, in_specs=None, scratch=()):
    return pl.pallas_call(
        kernel,
        out_shape=out_shape,
        in_specs=in_specs or [pl.BlockSpec()] * len(args),
        scratch_shapes=list(scratch),
        compiler_params=pltpu.CompilerParams(vmem_limit_bytes=limit * 1024 * 1024),
    )(*args)


def shape(dims, dtype):
    return jax.ShapeDtypeStruct(dims, dtype)


def in_hbm(value):
    return pltpu.with_memory_space_constraint(value, pltpu.HBM)


def in_vmem(value):
    return pltpu.with_memory_space_constraint(value, pltpu.VMEM)


def main_call(arrived, prepared, **options):
    def main(*refs):
        main_kernel(*refs, **options)

    return call(
        main,
        shape((16, 8, LANES), F32),
        (arrived,) + tuple(in_vmem(each) for each in prepared),
        MAIN_LIMIT,
        [pl.BlockSpec()] + [IN_VMEM] * len(HELD),
        [
            pltpu.VMEM((5, WINDOW, WIDTH, LANES), BF16),
            pltpu.VMEM((CELL_PAIRS, 64, LANES), F32),
            pltpu.VMEM((32, LANES), F32),
        ],
    )


def shards(
    member_predictors,
    member_skill_logit,
    opening_filter,
    opening_bias,
    following_filter,
    layer_norm_scales,
    query_key_value_weight,
    attention_output_weight,
    upward_weight,
    downward_weight,
    closing_norm_scale,
    readout_weight,
):
    own = member_predictors.reshape(LANES, LANES)
    mems, sps = lax.axis_size("mem"), lax.axis_size("sp")
    swap = []
    for i in range(1, sps - 2, 2):
        swap += [(i, i + 1), (i + 1, i)]
    other = lax.ppermute(own, "sp", swap)
    part = call(
        pack_own_kernel,
        shape((16, 16, LANES), BF16),
        (in_hbm(own), in_hbm(member_skill_logit.reshape(16, LANES))),
        PACK_LIMIT,
    )
    message = call(pack_other_kernel, shape((16, 32, LANES), BF16), (other, part), PACK_LIMIT)
    groups = [
        [m * sps + 2 * k + s for s in range(2) for m in range(mems)] for k in range(sps // 2)
    ]

    def exchange(value):
        return lax.all_to_all(
            value, ("mem", "sp"), 0, 0, tiled=True, axis_index_groups=groups
        )

    arrived = exchange(message)
    prepared = call(
        prepare_kernel,
        tuple(shape(*each) for each in HELD),
        tuple(
            in_hbm(each)
            for each in (
                opening_filter,
                opening_bias.reshape(1, WIDTH),
                following_filter,
                layer_norm_scales.reshape(2 * LAYERS, WIDTH),
                closing_norm_scale.reshape(1, WIDTH),
                query_key_value_weight,
                attention_output_weight,
                upward_weight,
                downward_weight,
                readout_weight.T,
            )
        ),
        PREPARE_LIMIT,
    )

    result = main_call(arrived, prepared, pairs=8, lag=(1, 1, 2, 1))
    got = exchange(result)
    output = call(unpack_kernel, shape((8, 4, LANES), F32), (got, own), UNPACK_LIMIT)
    return output.reshape(8, OUT_FIELDS, 2, LANES)


def solution(mesh):
    in_specs = (
        P("mem", None, "sp", None),
        P("mem", "sp", None),
        P(),
        P(),
        P(),
        P(),
        P(),
        P(),
        P(),
        P(),
        P(),
        P(),
    )
    out_specs = P("mem", None, "sp", None)
    return jax.shard_map(shards, mesh=mesh, in_specs=in_specs, out_specs=out_specs, check_vma=False)
```

```python
import math

import jax
import jax.numpy as jnp
from jax import lax
from jax.experimental import pallas as pl
from jax.experimental.pallas import tpu as pltpu
from jax.sharding import PartitionSpec as P

LAYERS = 2
WIDTH = 128
FF = 512
FIELDS = 8
OUT_FIELDS = 2
LANES = 128
SLOT = 16
COLUMNS = 8
WINDOW = COLUMNS + 2
CELL_PAIRS = 2 * COLUMNS
EPS = 1e-05
LOG2E = math.log2(math.e)
GELU_A = math.sqrt(2.0 / math.pi)
GELU_B = GELU_A * 0.044715

PACK_LIMIT = 8
MAIN_LIMIT = 40
PREPARE_LIMIT = 24
UNPACK_LIMIT = 8

F32 = jnp.float32
BF16 = jnp.bfloat16
NT = (((1,), (1,)), ((), ()))


def iota(shape, dim):
    return lax.broadcasted_iota(jnp.int32, shape, dim)


def matmul(a, b):
    return jnp.dot(a, b, preferred_element_type=F32)


def exact(condition):
    return condition.astype(F32).astype(BF16)


def gelu(half):
    return half + half * jnp.tanh(half * (2.0 * GELU_A + 8.0 * GELU_B * (half * half)))


def pack(rows, logits, store):
    i = iota((LANES, LANES), 0)
    k = iota((LANES, LANES), 1)
    order = exact(k == (i % 8) * 16 + (i // 16) * 2 + (i // 8) % 2)
    c = iota((LANES, 2 * LANES), 0)
    lane = iota((LANES, 2 * LANES), 1)
    dest = lane // SLOT
    j = lane % SLOT
    pick = exact((c == COLUMNS * dest - 2 + j) & (j < 12))
    if logits is not None:
        li = iota((16, 16), 0)
        lk = iota((16, 16), 1)
        order_logit = exact(lk == (li % 8) * 2 + li // 8)
        stretch = exact((c == COLUMNS * dest + j) & (j < COLUMNS))
        logits = matmul(matmul(order_logit, logits).astype(BF16), stretch)
    spot = iota((16, LANES), 1) % SLOT == 12
    masks = [(iota((16, LANES), 1) // SLOT // (1 << bit)) % 2 == 0 for bit in range(3)]
    picked = matmul(matmul(order, rows).astype(BF16), pick)
    for q in range(2):
        cut = slice(q * LANES, (q + 1) * LANES)
        blocks = []
        for f in range(FIELDS):
            block = picked[f * 16 : f * 16 + 16, cut]
            if logits is not None:
                block = jnp.where(spot, pltpu.roll(logits[:, cut], 12 - f, 1), block)
            blocks.append(block)
        for bit in range(3):
            step = 1 << bit
            shift = SLOT * step
            for f in range(FIELDS):
                if f & step == 0:
                    first, other = blocks[f], blocks[f + step]
                    blocks[f] = jnp.where(masks[bit], first, pltpu.roll(other, shift, 1))
                    blocks[f + step] = jnp.where(
                        masks[bit], pltpu.roll(first, LANES - shift, 1), other
                    )
        for n in range(8):
            store(8 * q + n, blocks[n].astype(BF16))


def pack_own_kernel(own_ref, logit_ref, out_ref, fields_ref):
    def store(n, value):
        out_ref[n] = value

    i = iota((32, LANES), 0)
    k = iota((32, LANES), 1)
    fields_ref[...] = matmul(exact(k == (i % 8) * 16 + i // 8), own_ref[...])
    pack(own_ref[...], logit_ref[...], store)


def pack_other_kernel(other_ref, part_ref, out_ref):
    out_ref[:, :16, :] = part_ref[...]

    def store(n, value):
        out_ref[n, 16:, :] = value

    pack(other_ref[...], None, store)


def prepare_kernel(
    opening_ref, bias_ref, following_ref, scales_ref, closing_ref, qkv_ref, out_w_ref, up_w_ref,
    down_w_ref, readout_ref,
    band_ref, bias_out, following_out, scales_out, qkv_out, out_w_out, up_w_out, down_w_out,
    readout_out,
):
    def flip(value):
        return value.astype(F32).T.astype(BF16)

    def column(row):
        return jnp.broadcast_to(row, (LANES, LANES)).T

    t = iota((72, 3 * LANES), 0)
    lane = iota((72, 3 * LANES), 1)
    tap = t // 8
    place = exact(
        (lane // LANES == tap // 3)
        & ((lane % LANES) // SLOT == t % 8)
        & (lane % SLOT == tap % 3)
    )
    flat = opening_ref[...].astype(F32).reshape(72, WIDTH)
    base = 0.5 * matmul(flat.T.astype(BF16), place)
    for c in range(WINDOW):
        for d in range(3):
            piece = base[:, d * LANES : (d + 1) * LANES]
            if c:
                piece = pltpu.roll(piece, c, 1)
            band_ref[c * WIDTH : (c + 1) * WIDTH, d * LANES : (d + 1) * LANES] = piece.astype(BF16)
    bias_out[...] = column(0.5 * bias_ref[...])
    for tap in range(9):
        following_out[:, tap * WIDTH : (tap + 1) * WIDTH] = flip(following_ref[tap])
    for layer in range(LAYERS):
        for n in range(2):
            scales_out[2 * layer + n] = column(scales_ref[2 * layer + n : 2 * layer + n + 1])
        for n in range(3):
            qkv_out[layer, n * WIDTH : (n + 1) * WIDTH] = flip(
                qkv_ref[layer, :, n * WIDTH : (n + 1) * WIDTH]
            )
        out_w_out[layer] = flip(out_w_ref[layer])
        for n in range(FF // WIDTH):
            cut = slice(n * WIDTH, (n + 1) * WIDTH)
            up_w_out[layer, cut] = flip(0.5 * up_w_ref[layer, :, cut].astype(F32))
            down_w_out[layer, :, cut] = flip(down_w_ref[layer, cut])
    scales_out[2 * LAYERS] = column(closing_ref[...])
    turned = readout_ref[...].astype(F32)
    readout_out[...] = jnp.concatenate(
        [turned, jnp.zeros((16 - OUT_FIELDS, WIDTH), F32)], axis=0
    ).astype(BF16)


def main_kernel(message_ref, *refs, pairs, lag):
    held_refs, refs = refs[: len(HELD)], refs[len(HELD) :]
    result_ref, first_ref, logit_ref, read_ref = refs
    (
        band_ref, bias_ref, following_ref, scales_ref, qkv_ref, out_w_ref, up_w_ref, down_w_ref,
        readout_ref,
    ) = held_refs
    mem = lax.axis_index("mem")
    sp = lax.axis_index("sp")
    low = iota((WIDTH, LANES), 1) < 64

    rows = []
    for source, slot in ((0, 1), (0, 0), (1, 0), (1, 1)):
        block = message_ref[source * 8 : source * 8 + 8, slot * 16 : slot * 16 + 16, :]
        block = block.astype(F32).reshape(8, 2, 8, LANES)
        for r in range(2):
            rows.append(block[:, r].reshape(64, LANES))
    for p in range(CELL_PAIRS):
        q, c = p // COLUMNS, p % COLUMNS
        lane = c * SLOT + 12
        spread = jnp.concatenate(
            [
                jnp.broadcast_to(rows[2 + 2 * q + r][:, lane : lane + 1], (64, 64))
                for r in range(2)
            ],
            axis=1,
        )
        logit_ref[p] = spread * LOG2E
    taken = [row.astype(BF16) for row in rows]
    window = jnp.concatenate(
        [jnp.concatenate(taken[d : d + 6], axis=0) for d in range(3)], axis=1
    )
    chip = sp // 2
    block = (sp % 2) * lax.axis_size("mem") + mem
    top = jnp.where(low & (chip == 0), 0.0, 1.0)
    bottom = jnp.where(low | (chip < lax.axis_size("sp") // 2 - 1), 1.0, 0.0)
    left = jnp.where(block > 0, 1.0, 0.0)
    right = jnp.where(block < 2 * lax.axis_size("mem") - 1, 1.0, 0.0)
    bias = bias_ref[...]

    for start in range(0, WINDOW, 2):
        summed = lax.dot_general(
            band_ref[start * WIDTH : (start + 2) * WIDTH],
            window,
            NT,
            preferred_element_type=F32,
        )
        for n in range(2):
            c = start + n
            two = []
            for t, keep in enumerate((top, None, bottom)):
                part = gelu(
                    summed[n * WIDTH : (n + 1) * WIDTH, t * LANES : (t + 1) * LANES] + bias
                )
                if keep is not None:
                    part = part * keep
                if c in (0, WINDOW - 1):
                    part = part * (right if c else left)
                two.append(part)
            turned = [pltpu.roll(part, 64, 1) for part in two]
            for t in range(3):
                first_ref[2 * t, c] = two[t].astype(BF16)
            for t in range(2):
                first_ref[2 * t + 1, c] = jnp.where(low, turned[t], turned[t + 1]).astype(BF16)

    key_mask = exact(
        iota((256, WIDTH), 0) // 64 == (iota((256, WIDTH), 1) // 16) % 4
    )
    value_mask = exact(iota((64, 256), 0) // 16 == iota((64, 256), 1) // 64)
    low_mask = exact(iota((WIDTH, LANES), 1) < 64)
    high_mask = exact(iota((WIDTH, LANES), 1) >= 64)
    scales = [scales_ref[n] for n in range(2 * LAYERS + 1)]

    def norm(stream, scale):
        parts = []
        for n in range(pairs):
            part = lanes_of(stream, n)
            centred = part - jnp.mean(part, 0, keepdims=True)
            variance = jnp.mean(centred * centred, 0, keepdims=True)
            parts.append((centred * lax.rsqrt(variance + EPS) * scale).astype(BF16))
        return jnp.concatenate(parts, axis=1)

    def lanes_of(value, n):
        return value[:, n * LANES : (n + 1) * LANES]

    groups = CELL_PAIRS // pairs
    streams = {}
    kept = {}

    def follow(group):
        taps = []
        for d in range(3):
            for e in range(3):
                parts = []
                for p in range(group * pairs, (group + 1) * pairs):
                    parts.append(first_ref[2 * (p // COLUMNS) + d, p % COLUMNS + e])
                taps.append(jnp.concatenate(parts, axis=1))
        stream = matmul(following_ref[...], jnp.concatenate(taps, axis=0))
        streams[group] = (stream + taps[4].astype(F32)).astype(BF16).astype(F32)

    def project(layer, group):
        normed = norm(streams[group], scales[2 * layer])
        kept[group, "triple"] = matmul(qkv_ref[layer], normed)

    def split(group, n):
        part = lanes_of(kept[group, "triple"], n)
        query = (part[:WIDTH] * (LOG2E / 4.0)).astype(BF16)
        cells = [query * low_mask, query * high_mask]
        zeros = jnp.zeros((64, LANES), BF16)
        query = jnp.concatenate(
            [
                jnp.concatenate([each for cell in cells for each in (cell[:64], zeros)], axis=0),
                jnp.concatenate([each for cell in cells for each in (zeros, cell[64:])], axis=0),
            ],
            axis=1,
        )
        key = part[WIDTH : 2 * WIDTH].T.astype(BF16)
        value = part[2 * WIDTH :]
        turned = pltpu.roll(value, 64, 1).astype(BF16)
        value = value.astype(BF16)
        values = [
            value * low_mask + turned * high_mask,
            turned * low_mask + value * high_mask,
        ]
        kept[group, n] = query, key, values

    def score(group, n):
        query, key, _ = kept[group, n]
        keys = jnp.concatenate(
            [
                jnp.concatenate([key[64 * r : 64 * r + 64]] * 4, axis=0) * key_mask
                for r in range(2)
            ],
            axis=1,
        )
        scores = matmul(keys, query)
        for half in range(2):
            kept[group, n, half] = lanes_of(scores, half)

    def soften(group, n, half):
        scores = kept[group, n, half].reshape(4, 64, LANES)
        scores = scores + logit_ref[group * pairs + n][None]
        raised = jnp.exp2(scores - jnp.max(scores, 1, keepdims=True))
        kept[group, n, half] = (
            raised.astype(BF16).reshape(256, LANES),
            1.0 / jnp.sum(raised, 1, keepdims=True),
        )

    def gather(group, n, half):
        raised, inverse = kept[group, n, half]
        spread = [
            jnp.concatenate([v[64 * half : 64 * half + 64]] * 2, axis=1) * value_mask
            for v in kept[group, n][2]
        ]
        found = matmul(jnp.concatenate(spread, axis=0), raised)
        picked = jnp.where(low[:64], found[:64], found[64:]).reshape(4, 16, LANES)
        kept[group, n, half] = (picked * inverse).reshape(64, LANES).astype(BF16)

    def attend(layer, group):
        attended = jnp.concatenate(
            [
                jnp.concatenate([kept[group, n, half] for half in range(2)], axis=0)
                for n in range(pairs)
            ],
            axis=1,
        )
        streams[group] = streams[group] + matmul(out_w_ref[layer], attended)

    def renorm(layer, group):
        kept[group, "normed"] = norm(streams[group], scales[2 * layer + 1])

    def widen(layer, group, q):
        cut = slice(q * WIDTH, (q + 1) * WIDTH)
        kept[group, "hidden", q] = matmul(up_w_ref[layer, cut], kept[group, "normed"])

    def bend(group, q):
        kept[group, "hidden", q] = gelu(kept[group, "hidden", q]).astype(BF16)

    def narrow(layer, group):
        hidden = jnp.concatenate(
            [kept[group, "hidden", q] for q in range(FF // WIDTH)], axis=0
        )
        streams[group] = streams[group] + matmul(down_w_ref[layer], hidden)

    def read(group):
        correction = matmul(readout_ref[...], norm(streams[group], scales[2 * LAYERS]))
        for n in range(pairs):
            for f in range(OUT_FIELDS):
                at = f * 16 + group * pairs + n
                read_ref[at : at + 1, :] = lanes_of(correction, n)[f : f + 1]

    issue = []
    slots = 2 * pairs
    for layer in range(LAYERS):
        for group in range(groups):
            base = (layer * groups + group) * slots

            def add(offset, step, *arguments, base=base):
                issue.append((base + offset, len(issue), step, arguments))

            if layer == 0:
                add(-2, follow, group)
            add(0, project, layer, group)
            at = 2
            for n in range(pairs):
                add(at + 2 * n, split, group, n)
                add(at + 2 * n + lag[0], score, group, n)
                for half in range(2):
                    k = at + 2 * n + half
                    add(k + lag[0] + lag[1], soften, group, n, half)
                    add(k + lag[0] + lag[1] + lag[2], gather, group, n, half)
            at = at + slots - 1 + sum(lag[:3]) + 1
            add(at, attend, layer, group)
            add(at + 1, renorm, layer, group)
            for q in range(4):
                add(at + 2 + q, widen, layer, group, q)
                add(at + 2 + q + lag[3], bend, group, q)
            at = at + 2 + 3 + lag[3] + 1
            add(at, narrow, layer, group)
            if layer == LAYERS - 1:
                add(at + 1, read, group)
    issue.sort(key=lambda entry: entry[:2])
    for _, _, step, arguments in issue:
        step(*arguments)

    turned = jnp.concatenate([read_ref[...], jnp.zeros((LANES - 32, LANES), F32)], axis=0).T
    result = turned[:64] + pltpu.roll(turned[64:], 32, 1)
    for s in range(2):
        result_ref[s * 8 : s * 8 + 8] = result.reshape(8, 8, LANES)


def unpack_kernel(got_ref, fields_ref, out_ref):
    fields = fields_ref[...]
    part = iota((8, LANES), 1) // COLUMNS
    odd = lax.axis_index("sp") % 2 == 1
    pieces = []
    for source in range(16):
        piece = got_ref[source]
        pieces.append(jnp.where(odd, pltpu.roll(piece, LANES - COLUMNS, 1), piece))
    for f in range(OUT_FIELDS):
        for r in range(2):
            n = 2 * f + r
            total = fields[n * 8 : n * 8 + 8]
            for source in range(16):
                shift = (COLUMNS * source - (r * 32 + f * 16)) % LANES
                piece = pieces[source]
                if shift:
                    piece = pltpu.roll(piece, shift, 1)
                total = total + jnp.where(part == source, piece, 0.0)
            out_ref[:, n, :] = total


HELD = (
    ((WINDOW * WIDTH, 3 * LANES), BF16),
    ((WIDTH, LANES), F32),
    ((WIDTH, 9 * WIDTH), BF16),
    ((2 * LAYERS + 1, WIDTH, LANES), F32),
    ((LAYERS, 3 * WIDTH, WIDTH), BF16),
    ((LAYERS, WIDTH, WIDTH), BF16),
    ((LAYERS, FF, WIDTH), BF16),
    ((LAYERS, WIDTH, FF), BF16),
    ((16, WIDTH), BF16),
)
IN_VMEM = pl.BlockSpec(memory_space=pltpu.VMEM)
IN_HBM = pl.BlockSpec(memory_space=pltpu.HBM)


def call(kernel, out_shape, args, limit, in_specs=None, scratch=()):
    return pl.pallas_call(
        kernel,
        out_shape=out_shape,
        in_specs=in_specs or [pl.BlockSpec()] * len(args),
        scratch_shapes=list(scratch),
        compiler_params=pltpu.CompilerParams(vmem_limit_bytes=limit * 1024 * 1024),
    )(*args)


def shape(dims, dtype):
    return jax.ShapeDtypeStruct(dims, dtype)


def in_hbm(value):
    return pltpu.with_memory_space_constraint(value, pltpu.HBM)


def in_vmem(value):
    return pltpu.with_memory_space_constraint(value, pltpu.VMEM)


def main_call(arrived, prepared, **options):
    def main(*refs):
        main_kernel(*refs, **options)

    return call(
        main,
        shape((16, 8, LANES), F32),
        (arrived,) + tuple(in_vmem(each) for each in prepared),
        MAIN_LIMIT,
        [pl.BlockSpec()] + [IN_VMEM] * len(HELD),
        [
            pltpu.VMEM((5, WINDOW, WIDTH, LANES), BF16),
            pltpu.VMEM((CELL_PAIRS, 64, LANES), F32),
            pltpu.VMEM((32, LANES), F32),
        ],
    )


def shards(
    member_predictors,
    member_skill_logit,
    opening_filter,
    opening_bias,
    following_filter,
    layer_norm_scales,
    query_key_value_weight,
    attention_output_weight,
    upward_weight,
    downward_weight,
    closing_norm_scale,
    readout_weight,
):
    own = member_predictors.reshape(LANES, LANES)
    mems, sps = lax.axis_size("mem"), lax.axis_size("sp")
    swap = []
    for i in range(1, sps - 2, 2):
        swap += [(i, i + 1), (i + 1, i)]
    other = lax.ppermute(own, "sp", swap)
    part, fields = call(
        pack_own_kernel,
        (shape((16, 16, LANES), BF16), shape((32, LANES), F32)),
        (in_hbm(own), in_hbm(member_skill_logit.reshape(16, LANES))),
        PACK_LIMIT,
    )
    message = call(pack_other_kernel, shape((16, 32, LANES), BF16), (other, part), PACK_LIMIT)
    groups = [
        [m * sps + 2 * k + s for s in range(2) for m in range(mems)] for k in range(sps // 2)
    ]

    def exchange(value):
        return lax.all_to_all(
            value, ("mem", "sp"), 0, 0, tiled=True, axis_index_groups=groups
        )

    arrived = exchange(message)
    prepared = call(
        prepare_kernel,
        tuple(shape(*each) for each in HELD),
        tuple(
            in_hbm(each)
            for each in (
                opening_filter,
                opening_bias.reshape(1, WIDTH),
                following_filter,
                layer_norm_scales.reshape(2 * LAYERS, WIDTH),
                closing_norm_scale.reshape(1, WIDTH),
                query_key_value_weight,
                attention_output_weight,
                upward_weight,
                downward_weight,
                readout_weight.T,
            )
        ),
        PREPARE_LIMIT,
    )

    result = main_call(arrived, prepared, pairs=8, lag=(1, 1, 2, 1))
    got = exchange(result)
    output = call(unpack_kernel, shape((8, 4, LANES), F32), (got, in_vmem(fields)), UNPACK_LIMIT)
    return output.reshape(8, OUT_FIELDS, 2, LANES)


def solution(mesh):
    in_specs = (
        P("mem", None, "sp", None),
        P("mem", "sp", None),
        P(),
        P(),
        P(),
        P(),
        P(),
        P(),
        P(),
        P(),
        P(),
        P(),
    )
    out_specs = P("mem", None, "sp", None)
    return jax.shard_map(shards, mesh=mesh, in_specs=in_specs, out_specs=out_specs, check_vma=False)
```
